256 devices in a mesh: group: 16 (over y, x), member: 16 (over z, core).
Axes of the slice: x: 4, y: 4, z: 8, core: 2. Of those that a mesh axis runs over, the one named last changes fastest.
Arguments:
- factor: float32 [16, 32, 768, 768], P('group', 'member'), as said below
- load: float32 [16, 32, 768], P('group', 'member'), may hold values from -6 to 6
- dof_map: int32 [16, 32, 768], P('group', 'member'), may hold values from 0 to 767, as said below
- dof_sign: int32 [16, 32, 768], P('group', 'member'), may hold values from -1 to 1, as said below
- live_count: int32 [16, 32], P('group', 'member'), may hold values from 384 to 768, as said below
- face_slot: int32 [16, 32, 4, 64], P('group', 'member'), may hold values from 0 to 767, as said below
- face_count: int32 [16, 32, 4], P('group', 'member'), may hold values from 0 to 64, as said below
- node_coord: int32 [16, 32, 3, 256], P('group', 'member'), may hold values from 0 to 15
- coarse_inverse: float32 [3072, 3072], P(('group', 'member')), as said below
Outputs:
- multipliers: float32 [16, 32, 768], P('group', 'member')
- projected: float32 [16, 32, 768], P('group', 'member')
The draws below stay inside these ranges and needn't reach their ends.
Inputs may be any that keep to these rules, and one draw needn't show every extreme that they name: `dof_map`: each subdomain's row is a permutation of the unknowns. `dof_sign`: every entry is -1 or 1. `live_count`: in each cluster, both subdomains of one device have 768 live multipliers and both subdomains of the device whose member index differs by a quarter of 32 have 384. `face_slot`: the slots of one subdomain are distinct and below its live_count; slot k of a face pairs with slot k of the partner's face. `face_count`: A face and its partner's face have the same count; faces at the ends of a cluster's chain and at the first and last cluster have 0, all others 1 or more. `factor`: lower triangular with a positive diagonal. `coarse_inverse`: symmetric positive definite.
All inputs are finite; a program needn't handle non-finite values.
Results may differ from the reference program's by a relative error of at most 0.0003.
Values sent between devices are 32-bit elements; how exact they have to be, the bound alone decides.
No kernel may reach another device: no remote copies, remote signals or barrier semaphores. Data moves between devices by JAX's collectives and lax.ppermute only.
A program may use at most 128 MiB of HBM per device.

```python
import jax
import jax.numpy as jnp
from jax import lax

NDOF = 768
NODES = 256
MODES = 6
CAP = 64
LIVE_MIN = 384
ITERS = 3
CLUSTERS = 16
SUBS = 32
COARSE = 3072


def geometry(key):
    key_list = jax.random.split(jax.random.fold_in(key, 4242), 12)
    count_subs = CLUSTERS * SUBS
    dof_maps = jax.vmap(lambda sub_key: jax.random.permutation(sub_key, NDOF))(jax.random.split(key_list[0], count_subs))
    dof_maps = dof_maps.astype(jnp.int32).reshape(CLUSTERS, SUBS, NDOF)
    dof_signs = (2 * jax.random.randint(key_list[1], (CLUSTERS, SUBS, NDOF), 0, 2) - 1).astype(jnp.int32)
    trials = jax.random.randint(key_list[2], (3, CLUSTERS, SUBS), 0, NDOF - LIVE_MIN + 1)
    live_counts = LIVE_MIN + jnp.min(trials, axis=0)
    members = SUBS // 2
    heavy_member = jax.random.randint(key_list[3], (CLUSTERS, 1), 0, members)
    light_member = (heavy_member + members // 2) % members
    member_index = (jnp.arange(SUBS, dtype=jnp.int32) // 2)[None, :]
    live_counts = jnp.where(member_index == heavy_member, NDOF, live_counts)
    live_counts = jnp.where(member_index == light_member, LIVE_MIN, live_counts).astype(jnp.int32)
    along_counts = jnp.minimum(jax.random.randint(key_list[4], (CLUSTERS, SUBS - 1), 1, CAP + 1), jax.random.randint(key_list[5], (CLUSTERS, SUBS - 1), 1, CAP + 1))
    forced_along = jax.random.randint(key_list[6], (), 0, CLUSTERS * (SUBS - 1))
    along_index = jnp.arange(CLUSTERS * (SUBS - 1), dtype=jnp.int32).reshape(CLUSTERS, SUBS - 1)
    along_counts = jnp.where(along_index == forced_along, CAP, along_counts)
    across_counts = jnp.minimum(jax.random.randint(key_list[7], (CLUSTERS - 1, SUBS), 1, CAP + 1), jax.random.randint(key_list[8], (CLUSTERS - 1, SUBS), 1, CAP + 1))
    forced_across = jax.random.randint(key_list[9], (), 0, (CLUSTERS - 1) * SUBS)
    across_index = jnp.arange((CLUSTERS - 1) * SUBS, dtype=jnp.int32).reshape(CLUSTERS - 1, SUBS)
    across_counts = jnp.where(across_index == forced_across, CAP, across_counts)
    zero_col = jnp.zeros((CLUSTERS, 1), jnp.int32)
    zero_row = jnp.zeros((1, SUBS), jnp.int32)
    face_counts = jnp.stack([jnp.concatenate([zero_col, along_counts], axis=1), jnp.concatenate([along_counts, zero_col], axis=1), jnp.concatenate([zero_row, across_counts], axis=0), jnp.concatenate([across_counts, zero_row], axis=0)], axis=2).astype(jnp.int32)
    positions = jnp.arange(NDOF, dtype=jnp.int32)
    raw_rank = jax.random.randint(key_list[10], (CLUSTERS, SUBS, NDOF), 0, 2 ** 20)
    sub_grid = jnp.arange(SUBS, dtype=jnp.int32)[None, :, None]
    clu_grid = jnp.arange(CLUSTERS, dtype=jnp.int32)[:, None, None]
    chosen_sub = 2 * heavy_member[0, 0]
    force_last = (clu_grid == 0) & (sub_grid == chosen_sub) & (positions[None, None, :] == NDOF - 1)
    raw_rank = jnp.where(force_last, 0, raw_rank)
    scores = raw_rank * NDOF + positions
    scores = jnp.where(positions[None, None, :] < live_counts[:, :, None], scores, 2000000000 + positions)
    ordering = jnp.argsort(scores, axis=2, stable=True).astype(jnp.int32)
    slot_list = ordering[:, :, :4 * CAP].reshape(CLUSTERS, SUBS, 4, CAP)
    coordinates = jax.random.randint(key_list[11], (CLUSTERS, SUBS, 3, NODES), 0, 16).astype(jnp.int32)
    return (dof_maps, dof_signs, live_counts, face_counts, slot_list, coordinates)


def draw_dof_map(key, part):
    return geometry(key)[0]


def draw_dof_sign(key, part):
    return geometry(key)[1]


def draw_live_count(key, part):
    return geometry(key)[2]


def draw_face_count(key, part):
    return geometry(key)[3]


def draw_face_slot(key, part):
    return geometry(key)[4]


def draw_node_coord(key, part):
    return geometry(key)[5]


def draw_factor(key, part):
    key_diag, key_lower, key_band, key_sign = jax.random.split(jax.random.fold_in(key, 9100), 4)
    diag_log = jax.random.uniform(key_diag, (CLUSTERS, SUBS, NDOF), jnp.float32, jnp.log(2.5), jnp.log(7.5))
    rough = jax.random.normal(key_lower, (CLUSTERS, SUBS, NDOF, NDOF), jnp.float32)
    band_size = jax.random.uniform(key_band, (CLUSTERS, SUBS, NDOF), jnp.float32, 0.9, 0.97)
    band_sign = (2 * jax.random.randint(key_sign, (CLUSTERS, SUBS, NDOF), 0, 2) - 1).astype(jnp.float32)
    below = jnp.eye(NDOF, k=-1, dtype=jnp.float32)
    band_part = (band_sign * band_size)[..., :, None] * below
    lower_part = jnp.tril(rough, -1) * (0.35 / jnp.sqrt(float(NDOF)))
    unit_lower = lower_part + band_part + jnp.eye(NDOF, dtype=jnp.float32)
    return jnp.exp(diag_log)[..., :, None] * unit_lower


def draw_coarse_inverse(key, part):
    key_rate, key_gain = jax.random.split(jax.random.fold_in(key, 7300))
    subs_total = CLUSTERS * SUBS
    rates = jnp.exp(jax.random.uniform(key_rate, (MODES,), jnp.float32, jnp.log(0.5), jnp.log(3.0)))
    gains = jnp.exp(jax.random.uniform(key_gain, (COARSE,), jnp.float32, jnp.log(0.6), jnp.log(1.6)))
    index = jnp.arange(COARSE, dtype=jnp.int32)
    sub_index = (index // MODES).astype(jnp.float32)
    mode_index = index % MODES
    same_mode = (mode_index[:, None] == mode_index[None, :]).astype(jnp.float32)
    distance = jnp.abs(sub_index[:, None] - sub_index[None, :]) / float(subs_total)
    rate_row = rates[mode_index][:, None]
    kernel = jnp.exp(-rate_row * distance) * same_mode
    scale = 4.0 / (float(NDOF) * jnp.sqrt(float(subs_total)))
    return scale * gains[:, None] * gains[None, :] * kernel


def shard_levels(key, dims, cuts, low, high):
    loudness, own = 1.0, jax.random.fold_in(key, 6)
    for axis_at, parts in cuts:
        draws = jnp.exp(jax.random.uniform(jax.random.fold_in(own, axis_at), (parts,), jnp.float32, low / len(cuts), high / len(cuts)))
        loudness = loudness * jnp.repeat(draws, dims[axis_at] // parts).reshape([-1 if axis == axis_at else 1 for axis in range(len(dims))])
    return loudness


def normal_values(own_key, shape, scale, most, cuts=(), held_as=jnp.bfloat16):
    loudness = shard_levels(own_key, shape, cuts, -0.22, 0.18) if cuts else 1.0
    values = jax.random.normal(own_key, shape, jnp.float32) * scale * loudness
    return jnp.minimum(jnp.maximum(values, -most), most).astype(held_as)


def setup_inputs(seed: int = 0) -> dict:
    arg_keys = jax.random.split(jax.random.key(seed), 10)
    return {
        "factor": draw_factor(jax.random.fold_in(arg_keys[9], 71), 0),
        "load": normal_values(arg_keys[1], (CLUSTERS, SUBS, NDOF), 1.0, 6.0, ((0, 16), (1, 16)), jnp.float32),
        "dof_map": draw_dof_map(jax.random.fold_in(arg_keys[9], 71), 0),
        "dof_sign": draw_dof_sign(jax.random.fold_in(arg_keys[9], 71), 0),
        "live_count": draw_live_count(jax.random.fold_in(arg_keys[9], 71), 0),
        "face_slot": draw_face_slot(jax.random.fold_in(arg_keys[9], 71), 0),
        "face_count": draw_face_count(jax.random.fold_in(arg_keys[9], 71), 0),
        "node_coord": draw_node_coord(jax.random.fold_in(arg_keys[9], 71), 0),
        "coarse_inverse": draw_coarse_inverse(jax.random.fold_in(arg_keys[9], 71), 0),
    }


highest = lax.Precision.HIGHEST
half_span = 8.0

def rigid_modes(node_coord):
    position = (node_coord.astype(jnp.float32) - half_span) / half_span
    spread = jnp.repeat(position, 3, axis=-1)
    component = jnp.arange(spread.shape[-1], dtype=jnp.int32) % 3
    first = (component == 0).astype(spread.dtype)
    second = (component == 1).astype(spread.dtype)
    third = (component == 2).astype(spread.dtype)
    coord_x = spread[..., 0, :]
    coord_y = spread[..., 1, :]
    coord_z = spread[..., 2, :]
    unit_row = jnp.ones_like(coord_x)
    return jnp.stack([first * unit_row, second * unit_row, third * unit_row, third * coord_y - second * coord_z, first * coord_z - third * coord_x, second * coord_x - first * coord_y], axis=-2)

def add_into(values, slot_list, amounts):
    flat_values = values.reshape(-1, values.shape[-1])
    rows = flat_values.shape[0]
    result = jax.vmap(lambda row_values, row_slots, row_amounts: row_values.at[row_slots].add(row_amounts))(flat_values, slot_list.reshape(rows, -1), amounts.reshape(rows, -1))
    return result.reshape(values.shape)

def reference(factor, load, dof_map, dof_sign, live_count, face_slot, face_count, node_coord, coarse_inverse):
    positions = jnp.arange(NDOF, dtype=jnp.int32)
    live_mask = positions[None, None, :] < live_count[:, :, None]
    signed = jnp.where(live_mask, dof_sign, 0).astype(jnp.float32)
    count_subs = CLUSTERS * SUBS
    panels = factor.reshape(count_subs, NDOF, NDOF)

    def one_dual(inputs):
        panel_matrix, mapping, sign_row = inputs
        inverse = lax.linalg.triangular_solve(panel_matrix, jnp.eye(NDOF, dtype=panel_matrix.dtype), left_side=True, lower=True)
        columns = jnp.take(inverse, mapping, axis=1) * sign_row[None, :]
        return jnp.dot(columns.T, columns, precision=highest)
    dual_all = lax.map(one_dual, (panels, dof_map.reshape(count_subs, NDOF), signed.reshape(count_subs, NDOF)))
    dual_all = dual_all.reshape(CLUSTERS, SUBS, NDOF, NDOF)

    def one_gap(inputs):
        panel_matrix, load_row = inputs
        forward = lax.linalg.triangular_solve(panel_matrix, load_row[:, None], left_side=True, lower=True)
        backward = lax.linalg.triangular_solve(panel_matrix, forward, left_side=True, lower=True, transpose_a=True)
        return backward[:, 0]
    displaced = lax.map(one_gap, (panels, load.reshape(count_subs, NDOF))).reshape(CLUSTERS, SUBS, NDOF)
    gap_local = jnp.take_along_axis(displaced, dof_map, axis=2) * signed
    mode_table = rigid_modes(node_coord)
    rigid_rows = jnp.take_along_axis(mode_table, jnp.broadcast_to(dof_map[:, :, None, :], mode_table.shape), axis=3)
    rigid_rows = rigid_rows * signed[:, :, None, :]
    coarse_rhs = jnp.einsum('gsai,gsi->gsa', mode_table, load, precision=highest)
    slot_used = (jnp.arange(CAP, dtype=jnp.int32)[None, None, None, :] < face_count[..., None]).astype(jnp.float32)
    flat_slots = face_slot.reshape(CLUSTERS, SUBS, 4 * CAP)
    shared = add_into(jnp.zeros_like(gap_local), flat_slots, slot_used.reshape(CLUSTERS, SUBS, 4 * CAP))
    weight = live_mask.astype(jnp.float32) * (1.0 - 0.5 * shared)

    def assemble(values):
        outgoing = jnp.take_along_axis(values, flat_slots, axis=2).reshape(CLUSTERS, SUBS, 4, CAP) * slot_used
        empty_row = jnp.zeros_like(outgoing[:, :1, 0])
        from_left = jnp.concatenate([empty_row, outgoing[:, :-1, 1]], axis=1)
        from_right = jnp.concatenate([outgoing[:, 1:, 0], empty_row], axis=1)
        empty_col = jnp.zeros_like(outgoing[:1, :, 0])
        from_below = jnp.concatenate([empty_col, outgoing[:-1, :, 3]], axis=0)
        from_above = jnp.concatenate([outgoing[1:, :, 2], empty_col], axis=0)
        incoming = jnp.stack([from_left, from_right, from_below, from_above], axis=2) * slot_used
        return add_into(values, flat_slots, incoming.reshape(CLUSTERS, SUBS, 4 * CAP))

    def inner(left_field, right_field):
        return jnp.sum(weight * left_field * right_field)

    def apply_inverse(coarse):
        return jnp.dot(coarse_inverse, coarse.reshape(COARSE), precision=highest).reshape(CLUSTERS, SUBS, MODES)

    def spread_modes(alpha):
        return jnp.einsum('gsaj,gsa->gsj', rigid_rows, alpha, precision=highest)

    def project(values):
        coarse = jnp.einsum('gsaj,gsj->gsa', rigid_rows, values, precision=highest)
        return values - assemble(spread_modes(apply_inverse(coarse)))

    def apply_dual(values):
        return jnp.einsum('gsij,gsj->gsi', dual_all, values, precision=highest)
    multipliers = assemble(spread_modes(apply_inverse(coarse_rhs)))
    residual = assemble(gap_local - apply_dual(multipliers))
    projected = project(residual)
    direction = projected
    norm_now = inner(projected, projected)
    for iteration in range(ITERS):
        image_vec = assemble(apply_dual(direction))
        step_size = norm_now / inner(direction, image_vec)
        multipliers = multipliers + step_size * direction
        residual = residual - step_size * image_vec
        projected = project(residual)
        norm_next = inner(projected, projected)
        direction = projected + norm_next / norm_now * direction
        norm_now = norm_next
    return (multipliers, projected)
```

```python
import jax
import jax.numpy as jnp
from jax import lax
from jax.experimental import pallas as pl
from jax.experimental.pallas import tpu as pltpu
from jax.sharding import PartitionSpec as P

ITERS = 3
ND = 768
LN = 128
NCH = ND // LN
DEV = 256
F32 = jnp.float32
BF = jnp.bfloat16
HI = lax.Precision.HIGHEST
NT = (((1,), (1,)), ((), ()))


def iota(shape, dim):
    return lax.broadcasted_iota(jnp.int32, shape, dim)


def tables_kernel(
    load_ref, map_ref, sign_ref, live_ref, slot_ref, used_ref, node_ref,
    tt_ref, qt_ref, rface_ref, own_ref, aux_ref, pay_ref,
):
    lane8 = iota((8, LN), 1)
    sub8 = iota((8, LN), 0)
    row = jnp.zeros((1, LN), F32)
    dim = iota((1, ND), 1).astype(F32)
    node = jnp.floor((dim + 0.5) * (1.0 / 3.0))
    comp = dim - 3.0 * node
    first = (comp == 0.0).astype(F32)
    second = (comp == 1.0).astype(F32)
    third = (comp == 2.0).astype(F32)
    delta = iota((256, ND), 1) - 3 * iota((256, ND), 0)
    rep = jnp.where((delta >= 0) & (delta < 3), 1.0, 0.0).astype(BF)
    for s in range(2):
        live = iota((1, ND), 1) < live_ref[s]
        live_f = jnp.where(live, 1.0, 0.0)
        sgn = jnp.where(live, sign_ref[s : s + 1, :].astype(F32), 0.0)
        dof = map_ref[s : s + 1, :]
        dof_f = dof.astype(F32)
        high = jnp.floor(dof_f * (1.0 / 32.0))
        low = dof_f - 32.0 * high
        part = iota((8, ND), 0)
        lhs = jnp.where(part == 0, high, jnp.where(part == 1, low, jnp.where(part == 2, sgn, 0.0)))
        slots = slot_ref[s : s + 1, :]
        used = used_ref[s : s + 1, :] > 0
        hit = jnp.where((iota((ND, 256), 0) == slots) & used, 1.0, 0.0).astype(BF)
        got = jnp.dot(lhs.astype(BF), hit, preferred_element_type=F32)
        dk = (32.0 * got[0:1, :] + got[1:2, :]).astype(jnp.int32)
        sk = got[2:3, :]
        tt = jnp.where(iota((ND, 256), 0) == dk, sk, 0.0)
        tt_b = tt.astype(BF)
        tt_ref[s] = tt_b
        qt = jnp.where(iota((ND, ND), 0) == dof, 1.0, 0.0).astype(BF)
        qt_ref[s] = qt
        mask = lax.dot_general(
            jnp.broadcast_to(live_f, (8, ND)).astype(BF), qt, NT, preferred_element_type=F32
        )[0:1, :]
        count = lax.dot_general(
            jnp.ones((8, 256), BF), jnp.abs(tt).astype(BF), NT, preferred_element_type=F32
        )[0:1, :]
        aux_ref[s : s + 1, :] = mask
        aux_ref[2 + s : 3 + s, :] = mask * (1.0 - 0.5 * count)
        aux_ref[4 + s : 5 + s, :] = sgn
        aux_ref[6 + s : 7 + s, :] = jnp.zeros((1, ND), F32)
        position = (node_ref[s].astype(F32) - 8.0) * 0.125
        spread = jnp.dot(position.astype(BF), rep, preferred_element_type=F32)
        cx = spread[0:1, :]
        cy = spread[1:2, :]
        cz = spread[2:3, :]
        rows = (
            first, second, third,
            third * cy - second * cz,
            first * cz - third * cx,
            second * cx - first * cy,
        )
        modes = jnp.zeros((8, ND), F32)
        for a in range(6):
            modes = jnp.where(part == a, rows[a], modes)
        own_ref[s] = modes * mask
        rface_ref[s] = jnp.dot(modes.astype(BF), tt_b, preferred_element_type=F32)
        e = jnp.sum(modes * load_ref[s : s + 1, :], axis=1, keepdims=True)
        row = row + jnp.sum(jnp.where(lane8 == sub8 + 8 * s, e, 0.0), axis=0, keepdims=True)
    pay_ref[...] = jnp.broadcast_to(row, (DEV, LN))


def half_masks(rows):
    return iota((rows, LN), 1) < 64


def pack_faces(o0, o1):
    lo = half_masks(o0.shape[0])
    o0l, o0h, o1l, o1h = o0[:, :LN], o0[:, LN:], o1[:, :LN], o1[:, LN:]
    to_gm = jnp.where(lo, o0h, pltpu.roll(o1h, 64, 1))
    to_gp = jnp.where(lo, pltpu.roll(o0h, 64, 1), o1h)
    return o0l, o1l, to_gm, to_gp


def spread_kernel(rf_ref, nb_ref, own_ref, tt_ref, ar_ref):
    lo = half_masks(8)
    zero = jnp.zeros((8, LN), F32)
    left, right, gm, gp = nb_ref[0], nb_ref[1], nb_ref[2], nb_ref[3]
    r0l, r1l = rf_ref[0][:, :LN], rf_ref[1][:, :LN]

    def both(a, b):
        return jnp.concatenate([a, b], axis=1)

    w0 = [
        both(zero, zero),
        both(pltpu.roll(jnp.where(lo, r1l, 0.0), 64, 1), zero),
        both(pltpu.roll(jnp.where(lo, 0.0, left), 64, 1), zero),
        both(zero, jnp.where(lo, gm, 0.0)),
        both(zero, jnp.where(lo, 0.0, pltpu.roll(gp, 64, 1))),
    ]
    w1 = [
        both(pltpu.roll(jnp.where(lo, 0.0, r0l), 64, 1), zero),
        both(zero, zero),
        both(pltpu.roll(jnp.where(lo, right, 0.0), 64, 1), zero),
        both(zero, jnp.where(lo, pltpu.roll(gm, 64, 1), 0.0)),
        both(zero, jnp.where(lo, 0.0, gp)),
    ]
    for s, w in ((0, w0), (1, w1)):
        table = jnp.concatenate(w, axis=0).astype(BF)
        ar_ref[s] = lax.dot_general(table, tt_ref[s], NT, preferred_element_type=F32)
        at = 8 * s
        ar_ref[s, at : at + 8, :] = own_ref[s]


def mm(a, b):
    return jnp.dot(a, b, precision=HI, preferred_element_type=F32)


def invert_kernel(l_ref, out_ref, n_ref, x_ref):
    ri = iota((LN, LN), 0)
    ci = iota((LN, LN), 1)
    eye = ri == ci
    below = ri > ci

    def block(s, i, j, width=LN):
        return l_ref[s, i * width : (i + 1) * width, j * width : (j + 1) * width]

    nblocks = 2 * NCH
    for k in range(nblocks):
        s, b = divmod(k, NCH)
        lb = block(s, b, b)
        diag = jnp.sum(jnp.where(eye, lb, 0.0), axis=1, keepdims=True)
        n = jnp.where(below, lb * (1.0 / diag), 0.0)
        n_ref[k] = n
        x_ref[k] = jnp.where(eye, 1.0, 0.0) - jnp.where((ri // 2) == (ci // 2), n, 0.0)
    size = 2
    while size < LN:
        pick = ((ri // (2 * size)) == (ci // (2 * size))) & ((ri // size) != (ci // size))
        inner = [mm(jnp.where(pick, n_ref[k], 0.0), x_ref[k]) for k in range(nblocks)]
        for k in range(nblocks):
            x = x_ref[k]
            x_ref[k] = x - mm(x, inner[k])
        size *= 2
    for k in range(nblocks):
        s, b = divmod(k, NCH)
        diag = jnp.sum(jnp.where(eye, block(s, b, b), 0.0), axis=0, keepdims=True)
        x_ref[k] = x_ref[k] * (1.0 / diag)
    zero = jnp.zeros((LN, LN), F32)
    big = {}
    for s in range(2):
        for q in range(NCH // 2):
            upper = x_ref[s * NCH + 2 * q]
            lower = x_ref[s * NCH + 2 * q + 1]
            corner = -mm(lower, mm(block(s, 2 * q + 1, 2 * q), upper))
            at = 2 * q * LN
            out_ref[s, at : at + LN, at : at + LN] = upper
            out_ref[s, at : at + LN, at + LN : at + 2 * LN] = zero
            out_ref[s, at + LN : at + 2 * LN, at : at + LN] = corner
            out_ref[s, at + LN : at + 2 * LN, at + LN : at + 2 * LN] = lower
    wd = 2 * LN

    def inv(s, i, j):
        return out_ref[s, i * wd : (i + 1) * wd, j * wd : (j + 1) * wd]

    for s in range(2):
        out_ref[s, wd : 2 * wd, 0:wd] = -mm(inv(s, 1, 1), mm(block(s, 1, 0, wd), inv(s, 0, 0)))
    for s in range(2):
        out_ref[s, 2 * wd : 3 * wd, wd : 2 * wd] = -mm(
            inv(s, 2, 2), mm(block(s, 2, 1, wd), inv(s, 1, 1))
        )
    for s in range(2):
        mid = mm(block(s, 2, 0, wd), inv(s, 0, 0)) + mm(block(s, 2, 1, wd), inv(s, 1, 0))
        out_ref[s, 2 * wd : 3 * wd, 0:wd] = -mm(inv(s, 2, 2), mid)


def split3(rows, total):
    idx = iota((total, rows[0].shape[1]), 0)
    out = jnp.zeros((total, rows[0].shape[1]), F32)
    for r, z in enumerate(rows):
        h = z.astype(BF).astype(F32)
        rest = z - h
        m = rest.astype(BF).astype(F32)
        l = rest - m
        out = jnp.where(idx == 3 * r, h, out)
        out = jnp.where(idx == 3 * r + 1, m, out)
        out = jnp.where(idx == 3 * r + 2, l, out)
    return out.astype(BF)


def solve(inv_ref, s, z):
    ys = []
    for b in range(NCH):
        acc = None
        for c in range(b + 1):
            term = inv_ref[s, b * LN : (b + 1) * LN, c * LN : (c + 1) * LN] * z[:, c * LN : (c + 1) * LN]
            acc = term if acc is None else acc + term
        ys.append(jnp.sum(acc, axis=1, keepdims=True))
    us = []
    for c in range(NCH):
        acc = None
        for b in range(c, NCH):
            term = inv_ref[s, b * LN : (b + 1) * LN, c * LN : (c + 1) * LN] * ys[b]
            acc = term if acc is None else acc + term
        us.append(jnp.sum(acc, axis=0, keepdims=True))
    return jnp.concatenate(us, axis=1)


def received_coarse(recv_ref):
    xt = jnp.transpose(recv_ref[:, 0:LN])

    def grp(i):
        return xt[8 * i : 8 * i + 8, :]

    h0 = grp(0) + pltpu.roll(grp(2), 1, 1) + pltpu.roll(grp(4), DEV - 16, 1) + pltpu.roll(grp(6), 16, 1)
    h1 = grp(1) + pltpu.roll(grp(3), DEV - 1, 1) + pltpu.roll(grp(5), DEV - 16, 1) + pltpu.roll(grp(7), 16, 1)
    sums = jnp.sum(grp(8), axis=1, keepdims=True)
    return h0, h1, sums


def project_rows(h0, h1, m_ref, ar_ref):
    acc = jnp.zeros((64, DEV), F32)
    for v in range(12):
        h = h0 if v < 6 else h1
        a = v % 6
        acc = acc + m_ref[:, v * DEV : (v + 1) * DEV] * h[a : a + 1, :]
    al = jnp.sum(acc, axis=1, keepdims=True)

    def grp(i):
        return al[8 * i : 8 * i + 8, :]

    a0 = jnp.concatenate([grp(0), grp(1), grp(3), grp(4), grp(6)], axis=0)
    a1 = jnp.concatenate([grp(0), grp(1), grp(2), grp(5), grp(7)], axis=0)
    w0 = jnp.sum(ar_ref[0] * a0, axis=0, keepdims=True)
    w1 = jnp.sum(ar_ref[1] * a1, axis=0, keepdims=True)
    return w0, w1


def tile_of(row):
    base = pl.multiple_of((row // 8) * 8, 8)
    return base, row - base


def face_row(recv_ref, row):
    base, offset = tile_of(row)
    tile = recv_ref[pl.ds(base, 8), LN : 2 * LN]
    return jnp.sum(jnp.where(iota((8, LN), 0) == offset, tile, 0.0), axis=0, keepdims=True)


def assembled(pos_ref, recv_ref, y, o, tt_ref):
    lo = half_masks(1)
    left, right, gm, gp = (face_row(recv_ref, pos_ref[i]) for i in range(4))
    o0l, o1l = o[0][:, :LN], o[1][:, :LN]
    in0 = jnp.concatenate(
        [pltpu.roll(jnp.where(lo, o1l, left), 64, 1), jnp.where(lo, gm, pltpu.roll(gp, 64, 1))], axis=1
    )
    in1 = jnp.concatenate(
        [pltpu.roll(jnp.where(lo, right, o0l), 64, 1), jnp.where(lo, pltpu.roll(gm, 64, 1), gp)], axis=1
    )
    out = []
    for s, inc in ((0, in0), (1, in1)):
        add = lax.dot_general(split3([inc], 8), tt_ref[s], NT, preferred_element_type=F32)
        out.append(y[s] + jnp.sum(add, axis=0, keepdims=True))
    return out


def send(pos_ref, pay_ref, y, tt_ref, ar_ref, dots):
    o = []
    cols = []
    for s in range(2):
        prod = jnp.dot(split3([y[s]], 8), tt_ref[s], preferred_element_type=F32)
        o.append(jnp.sum(prod, axis=0, keepdims=True))
        cols.append(jnp.sum(ar_ref[s] * y[s], axis=1, keepdims=True))
    c0, c1 = cols

    def grp(c, i):
        return c[8 * i : 8 * i + 8, :]

    cc = jnp.concatenate(
        [
            grp(c0, 0) + grp(c1, 0), grp(c0, 1) + grp(c1, 1), grp(c1, 2), grp(c0, 2),
            grp(c0, 3), grp(c1, 3), grp(c0, 4), grp(c1, 4),
        ],
        axis=0,
    )
    diag = iota((64, LN), 0) == iota((64, LN), 1)
    row = jnp.sum(jnp.where(diag, cc, 0.0), axis=0, keepdims=True)
    lane = iota((1, LN), 1)
    for i, value in enumerate(dots):
        row = jnp.where(lane == 64 + i, value, row)
    pay_ref[:, 0:LN] = jnp.broadcast_to(row, (DEV, LN))
    pay_ref[:, LN : 2 * LN] = jnp.zeros((DEV, LN), F32)
    to_left, to_right, to_gm, to_gp = pack_faces(o[0], o[1])
    for i, face in enumerate((to_left, to_right, to_gm, to_gp)):
        base, offset = tile_of(pos_ref[i])
        old = pay_ref[pl.ds(base, 8), LN : 2 * LN]
        pay_ref[pl.ds(base, 8), LN : 2 * LN] = jnp.where(iota((8, LN), 0) == offset, face, old)
    return o


def inner(a, b):
    return jnp.sum(a[0] * b[0] + a[1] * b[1], axis=1, keepdims=True)


def pair(ref, i):
    return [ref[i : i + 1, :], ref[i + 1 : i + 2, :]]


def put(ref, i, v):
    ref[i : i + 1, :] = v[0]
    ref[i + 1 : i + 2, :] = v[1]


LAM, PV, DV, IM, YD, YV = 0, 2, 4, 6, 8, 10


def begin_kernel(pos_ref, recv_ref, load_ref, inv_ref, tt_ref, ar_ref, m_ref, aux_ref, st_ref, o_ref, pay_ref):
    h0, h1, _ = received_coarse(recv_ref)
    lam = project_rows(h0, h1, m_ref, ar_ref)
    mask = pair(aux_ref, 0)
    y = [mask[s] * solve(inv_ref, s, load_ref[s : s + 1, :] - lam[s]) for s in range(2)]
    o = send(pos_ref, pay_ref, y, tt_ref, ar_ref, [])
    put(st_ref, LAM, lam)
    put(st_ref, YV, y)
    put(o_ref, 0, o)


def next_solve(pos_ref, pay_ref, inv_ref, tt_ref, ar_ref, aux_ref, p, d, yd):
    mask = pair(aux_ref, 0)
    weight = pair(aux_ref, 2)
    y = [mask[s] * solve(inv_ref, s, p[s]) for s in range(2)]
    wp = [weight[s] * p[s] for s in range(2)]
    dots = [inner(wp, p), inner(p, y)]
    if d is not None:
        dots += [inner(d, y), inner(p, yd)]
    o = send(pos_ref, pay_ref, y, tt_ref, ar_ref, dots)
    return y, o


def first_kernel(pos_ref, recv_ref, st_ref, o_ref, inv_ref, tt_ref, ar_ref, m_ref, aux_ref, st2_ref, o2_ref, pay_ref):
    h0, h1, _ = received_coarse(recv_ref)
    w = project_rows(h0, h1, m_ref, ar_ref)
    res = assembled(pos_ref, recv_ref, pair(st_ref, YV), pair(o_ref, 0), tt_ref)
    p = [res[s] - w[s] for s in range(2)]
    y, o = next_solve(pos_ref, pay_ref, inv_ref, tt_ref, ar_ref, aux_ref, p, None, None)
    put(st2_ref, LAM, pair(st_ref, LAM))
    put(st2_ref, PV, p)
    put(st2_ref, YV, y)
    put(o2_ref, 0, o)


def step_body(it, pos_ref, recv_ref, st_ref, o_ref, hs_ref, tt_ref, ar_ref, m_ref):
    h0, h1, sums = received_coarse(recv_ref)
    norm = sums[0:1, :]
    y = pair(st_ref, YV)
    p = pair(st_ref, PV)
    image = assembled(pos_ref, recv_ref, y, pair(o_ref, 0), tt_ref)
    if it == 0:
        d, yd, curve = p, y, sums[1:2, :]
    else:
        beta = norm / hs_ref[16:17, 0:1]
        curve = sums[1:2, :] + beta * (sums[2:3, :] + sums[3:4, :]) + beta * beta * hs_ref[17:18, 0:1]
        dold, iold, yold = pair(st_ref, DV), pair(st_ref, IM), pair(st_ref, YD)
        d = [p[s] + beta * dold[s] for s in range(2)]
        yd = [y[s] + beta * yold[s] for s in range(2)]
        image = [image[s] + beta * iold[s] for s in range(2)]
        h0 = h0 + beta * hs_ref[0:8, :]
        h1 = h1 + beta * hs_ref[8:16, :]
    step = norm / curve
    w = project_rows(h0, h1, m_ref, ar_ref)
    lam = pair(st_ref, LAM)
    lam = [lam[s] + step * d[s] for s in range(2)]
    pn = [p[s] - step * (image[s] - w[s]) for s in range(2)]
    return lam, pn, d, yd, image, h0, h1, norm, curve


def make_step(it):
    def step_kernel(
        pos_ref, recv_ref, st_ref, o_ref, hs_ref, inv_ref, tt_ref, ar_ref, m_ref, aux_ref,
        st2_ref, o2_ref, hs2_ref, pay_ref,
    ):
        lam, pn, d, yd, image, h0, h1, norm, curve = step_body(
            it, pos_ref, recv_ref, st_ref, o_ref, hs_ref, tt_ref, ar_ref, m_ref
        )
        y, o = next_solve(pos_ref, pay_ref, inv_ref, tt_ref, ar_ref, aux_ref, pn, d, yd)
        for at, v in ((LAM, lam), (PV, pn), (DV, d), (IM, image), (YD, yd), (YV, y)):
            put(st2_ref, at, v)
        put(o2_ref, 0, o)
        hs2_ref[0:8, :] = h0
        hs2_ref[8:16, :] = h1
        hs2_ref[16:17, :] = jnp.broadcast_to(norm, (1, DEV))
        hs2_ref[17:18, :] = jnp.broadcast_to(curve, (1, DEV))

    return step_kernel


def last_kernel(pos_ref, recv_ref, st_ref, o_ref, hs_ref, tt_ref, ar_ref, m_ref, aux_ref, qt_ref, lam_ref, p_ref):
    lam, pn = step_body(ITERS - 1, pos_ref, recv_ref, st_ref, o_ref, hs_ref, tt_ref, ar_ref, m_ref)[:2]
    for s in range(2):
        got = jnp.dot(split3([lam[s], pn[s]], 8), qt_ref[s], preferred_element_type=F32)
        sgn = aux_ref[4 + s : 5 + s, :]
        lam_ref[s : s + 1, :] = sgn * jnp.sum(got[0:3, :], axis=0, keepdims=True)
        p_ref[s : s + 1, :] = sgn * jnp.sum(got[3:6, :], axis=0, keepdims=True)


def sds(shape, dtype=F32):
    return jax.ShapeDtypeStruct(shape, dtype)


VM = pl.BlockSpec(memory_space=pltpu.VMEM)
SM = pl.BlockSpec(memory_space=pltpu.SMEM)


def call(kernel, outs, smem, *args, scratch=(), flops=0, name=None):
    specs = [SM if i in smem else VM for i in range(len(args))]
    return pl.pallas_call(
        kernel,
        out_shape=outs,
        in_specs=specs,
        out_specs=tuple(VM for _ in outs),
        scratch_shapes=list(scratch),
        name=name,
        compiler_params=pltpu.CompilerParams(vmem_limit_bytes=40 * 2**20),
        cost_estimate=pl.CostEstimate(flops=flops, transcendentals=0, bytes_accessed=2**20)
        if flops
        else None,
    )(*args)


def shards(factor, load, dof_map, dof_sign, live_count, face_slot, face_count, node_coord, coarse_inverse):
    axes = ("group", "member")
    g = lax.axis_index("group")
    m = lax.axis_index("member")
    me = g * 16 + m
    pos = jnp.stack(
        [
            jnp.where(m > 0, me - 1, me),
            jnp.where(m < 15, me + 1, me),
            jnp.where(g > 0, me - 16, me),
            jnp.where(g < 15, me + 16, me),
        ]
    ).astype(jnp.int32)
    loads = load[0]
    slots = face_slot[0].reshape(2, 256)
    used = (jnp.arange(64, dtype=jnp.int32)[None, None, :] < face_count[0][:, :, None]).astype(jnp.int32)
    used = used.reshape(2, 256)
    tt, qt, rface, own, aux, pay0 = call(
        tables_kernel,
        (
            sds((2, ND, 256), BF), sds((2, ND, ND), BF), sds((2, 8, 256)), sds((2, 8, ND)),
            sds((8, ND)), sds((DEV, LN)),
        ),
        (3,),
        loads, dof_map[0], dof_sign[0], live_count[0], slots, used, node_coord[0],
        name="tables",
    )

    def exchange(pay):
        return lax.all_to_all(pay, axes, 0, 0, tiled=True)

    recv0 = exchange(pay0)
    rows = coarse_inverse.reshape(12, DEV, 12).transpose(0, 2, 1).reshape(2, 6, 12 * DEV)
    rows = jnp.pad(rows, ((0, 0), (0, 2), (0, 0)))
    up = [(i, i + 1) for i in range(15)]
    down = [(i + 1, i) for i in range(15)]
    lo = jnp.arange(LN) < 64
    r0h, r1h = rface[0][:, LN:], rface[1][:, LN:]
    to_gm = jnp.where(lo, r0h, jnp.roll(r1h, 64, 1))
    to_gp = jnp.where(lo, jnp.roll(r0h, 64, 1), r1h)
    from_right = lax.ppermute(jnp.concatenate([rows[0], rface[0][:, :LN]], axis=1), "member", down)
    from_left = lax.ppermute(jnp.concatenate([rows[1], rface[1][:, :LN]], axis=1), "member", up)
    flat = rows.reshape(16, 12 * DEV)
    pad8 = jnp.zeros((8, LN), F32)
    from_gp = lax.ppermute(
        jnp.concatenate([flat, jnp.concatenate([to_gm, pad8], axis=0)], axis=1), "group", down
    )
    from_gm = lax.ppermute(
        jnp.concatenate([flat, jnp.concatenate([to_gp, pad8], axis=0)], axis=1), "group", up
    )
    (inv,) = call(
        invert_kernel,
        (sds((2, ND, ND)),),
        (),
        factor[0],
        scratch=[pltpu.VMEM((2 * NCH, LN, LN), F32), pltpu.VMEM((2 * NCH, LN, LN), F32)],
        flops=20_000_000_000,
        name="invert",
    )
    wide = 12 * DEV
    table = jnp.concatenate(
        [flat, from_right[:, :wide], from_left[:, :wide], from_gm[:, :wide], from_gp[:, :wide]], axis=0
    )
    near = jnp.stack(
        [from_left[:, wide:], from_right[:, wide:], from_gm[0:8, wide:], from_gp[0:8, wide:]]
    )
    (ar,) = call(spread_kernel, (sds((2, 40, ND)),), (), rface, near, own, tt, name="spread")
    st_s, o_s, hs_s, pay_s = sds((12, ND)), sds((2, 256)), sds((24, DEV)), sds((DEV, 2 * LN))
    st, o, pay = call(
        begin_kernel, (st_s, o_s, pay_s), (0,), pos, recv0, loads, inv, tt, ar, table, aux, name="begin"
    )
    st, o, pay = call(
        first_kernel, (st_s, o_s, pay_s), (0,), pos, exchange(pay), st, o, inv, tt, ar, table, aux,
        name="first",
    )
    hs = jnp.zeros((24, DEV), F32)
    for it in range(ITERS - 1):
        st, o, hs, pay = call(
            make_step(it), (st_s, o_s, hs_s, pay_s), (0,),
            pos, exchange(pay), st, o, hs, inv, tt, ar, table, aux, name=f"step{it}",
        )
    lam, proj = call(
        last_kernel, (sds((2, ND)), sds((2, ND))), (0,),
        pos, exchange(pay), st, o, hs, tt, ar, table, aux, qt, name="last",
    )
    return lam[None], proj[None]


def solution(mesh):
    return jax.shard_map(
        shards,
        mesh=mesh,
        in_specs=(
            P("group", "member", None, None),
            P("group", "member", None),
            P("group", "member", None),
            P("group", "member", None),
            P("group", "member"),
            P("group", "member", None, None),
            P("group", "member", None),
            P("group", "member", None, None),
            P(("group", "member"), None),
        ),
        out_specs=(P("group", "member", None), P("group", "member", None)),
        check_vma=False,
    )
```

```python
import jax
import jax.numpy as jnp
from jax import lax
from jax.experimental import pallas as pl
from jax.experimental.pallas import tpu as pltpu
from jax.sharding import PartitionSpec as P

ITERS = 3
ND = 768
LN = 128
NCH = ND // LN
DEV = 256
BASE = 16
F32 = jnp.float32
BF = jnp.bfloat16
NT = (((1,), (1,)), ((), ()))


def iota(shape, dim):
    return lax.broadcasted_iota(jnp.int32, shape, dim)


def coarse_kernel(load_hbm, node_hbm, modes_ref, pay_ref, load_ref, node_ref, sems):
    copies = [
        pltpu.make_async_copy(node_hbm, node_ref, sems.at[0]),
        pltpu.make_async_copy(load_hbm, load_ref, sems.at[1]),
    ]
    for c in copies:
        c.start()
    lane8 = iota((8, LN), 1)
    sub8 = iota((8, LN), 0)
    part = iota((8, ND), 0)
    row = jnp.zeros((1, LN), F32)
    dim = iota((1, ND), 1).astype(F32)
    node = jnp.floor((dim + 0.5) * (1.0 / 3.0))
    comp = dim - 3.0 * node
    first = (comp == 0.0).astype(F32)
    second = (comp == 1.0).astype(F32)
    third = (comp == 2.0).astype(F32)
    delta = iota((256, ND), 1) - 3 * iota((256, ND), 0)
    rep = jnp.where((delta >= 0) & (delta < 3), 1.0, 0.0).astype(BF)
    for c in copies:
        c.wait()
    for s in range(2):
        position = (node_ref[0, :, s, :].astype(F32) - 8.0) * 0.125
        spread = jnp.dot(position.astype(BF), rep, preferred_element_type=F32)
        cx = spread[0:1, :]
        cy = spread[1:2, :]
        cz = spread[2:3, :]
        rows = (
            first, second, third,
            third * cy - second * cz,
            first * cz - third * cx,
            second * cx - first * cy,
        )
        modes = jnp.zeros((8, ND), F32)
        for a in range(6):
            modes = jnp.where(part == a, rows[a], modes)
        modes_ref[s] = modes
        e = jnp.sum(modes * load_ref[0, s : s + 1, :], axis=1, keepdims=True)
        row = row + jnp.sum(jnp.where(lane8 == sub8 + 8 * s, e, 0.0), axis=0, keepdims=True)
    pay_ref[...] = jnp.broadcast_to(row, (DEV, LN))


def tables_kernel(
    modes_ref, load_hbm, map_hbm, sign_hbm, live_hbm, slot_hbm, count_hbm, coarse_hbm,
    tt_ref, qt_hbm, own_hbm, aux_ref, left_ref, right_ref, gm_ref, gp_ref,
    load_ref, map_ref, sign_ref, live_ref, slot_ref, count_ref, coarse_ref, own_ref, qt_ref, sems,
):
    copies = [
        pltpu.make_async_copy(src, dst, sems.at[i])
        for i, (src, dst) in enumerate(
            (
                (load_hbm, load_ref), (map_hbm, map_ref), (sign_hbm, sign_ref),
                (live_hbm, live_ref), (slot_hbm, slot_ref), (count_hbm, count_ref),
                (coarse_hbm, coarse_ref),
            )
        )
    ]
    for c in copies:
        c.start()
    part = iota((8, ND), 0)
    for c in copies[:-1]:
        c.wait()
    faces = []
    late = []
    for s in range(2):
        live = iota((1, ND), 1) < live_ref[0:1, s : s + 1]
        live_f = jnp.where(live, 1.0, 0.0)
        sgn = jnp.where(live, sign_ref[0, s : s + 1, :].astype(F32), 0.0)
        dof = map_ref[0, s : s + 1, :]
        dof_f = dof.astype(F32)
        high = jnp.floor(dof_f * (1.0 / 32.0))
        low = dof_f - 32.0 * high
        lhs = jnp.where(part == 0, high, jnp.where(part == 1, low, jnp.where(part == 2, sgn, 0.0)))
        pos64 = iota((1, 64), 1)
        slots = jnp.concatenate(
            [
                jnp.where(pos64 < count_ref[0, s : s + 1, f : f + 1], slot_ref[0, s, f : f + 1, :], -1)
                for f in range(4)
            ],
            axis=1,
        )
        hit = jnp.where(iota((ND, 256), 0) == slots, 1.0, 0.0).astype(BF)
        got = jnp.dot(lhs.astype(BF), hit, preferred_element_type=F32)
        dk = (32.0 * got[0:1, :] + got[1:2, :]).astype(jnp.int32)
        sk = got[2:3, :]
        tt = jnp.where(iota((ND, 256), 0) == dk, sk, 0.0)
        tt_b = tt.astype(BF)
        tt_ref[s] = tt_b
        qt = jnp.where(iota((ND, ND), 0) == dof, 1.0, 0.0).astype(BF)
        qt_ref[s] = qt
        qt_copy = pltpu.make_async_copy(qt_ref.at[s], qt_hbm.at[s], sems.at[8 + s])
        qt_copy.start()
        late.append(qt_copy)
        mask = lax.dot_general(
            jnp.broadcast_to(live_f, (8, ND)).astype(BF), qt, NT, preferred_element_type=F32
        )[0:1, :]
        count = lax.dot_general(
            jnp.ones((8, 256), BF), jnp.abs(tt).astype(BF), NT, preferred_element_type=F32
        )[0:1, :]
        aux_ref[s : s + 1, :] = mask
        aux_ref[2 + s : 3 + s, :] = mask * (1.0 - 0.5 * count)
        aux_ref[4 + s : 5 + s, :] = sgn
        aux_ref[6 + s : 7 + s, :] = load_ref[0, s : s + 1, :]
        modes = modes_ref[s]
        own_ref[s, 0:8, :] = modes * mask
        face = jnp.dot(modes.astype(BF), tt_b, preferred_element_type=F32)
        own_ref[s, 8:16, :] = jnp.concatenate([face, jnp.zeros((8, ND - 256), F32)], axis=1)
        faces.append(face)
    wide = 12 * DEV
    to_left, to_right, to_gm, to_gp = pack_faces(faces[0], faces[1])
    left_ref[:, wide:] = to_left
    right_ref[:, wide:] = to_right
    zero = jnp.zeros((8, LN), F32)
    gm_ref[0:8, wide:] = to_gm
    gp_ref[0:8, wide:] = to_gp
    gm_ref[8:16, wide:] = zero
    gp_ref[8:16, wide:] = zero
    own_copy = pltpu.make_async_copy(own_ref, own_hbm, sems.at[7])
    own_copy.start()
    late.append(own_copy)
    copies[-1].wait()
    perm = jnp.where(
        (iota((384, 384), 0) - 12 * (iota((384, 384), 1) % 32)) == iota((384, 384), 1) // 32, 1.0, 0.0
    ).astype(BF)
    keep = iota((8, 384), 0) < 6
    res = []
    for q in range(8):
        c = coarse_ref[:, 384 * q : 384 * (q + 1)]
        c16 = jnp.concatenate([c, jnp.zeros((4, 384), F32)], axis=0)
        up = jnp.where(keep, c16[0:8], 0.0)
        dn = jnp.where(keep, pltpu.roll(c16, 10, 0)[0:8], 0.0)
        both = jnp.concatenate([up, dn], axis=0)
        h = both.astype(BF)
        rest = both - h.astype(F32)
        m = rest.astype(BF)
        l = (rest - m.astype(F32)).astype(BF)
        got = jnp.dot(jnp.concatenate([h, m, l], axis=0), perm, preferred_element_type=F32)
        res.append(got[0:16] + got[16:32] + got[32:48])
    quarter = iota((16, LN), 1) // 32
    for v in range(12):
        for half in range(2):
            acc = None
            for i in range(4):
                src = res[4 * half + i][:, LN * (v // 4) : LN * (v // 4 + 1)]
                shift = (32 * (i - v % 4)) % LN
                src = pltpu.roll(src, shift, 1) if shift else src
                acc = src if acc is None else jnp.where(quarter == i, src, acc)
            at = v * DEV + half * LN
            left_ref[:, at : at + LN] = acc[0:8]
            right_ref[:, at : at + LN] = acc[8:16]
            gm_ref[:, at : at + LN] = acc
            gp_ref[:, at : at + LN] = acc
    for c in late:
        c.wait()


def half_masks(rows):
    return iota((rows, LN), 1) < 64


def pack_faces(o0, o1):
    lo = half_masks(o0.shape[0])
    o0l, o0h, o1l, o1h = o0[:, :LN], o0[:, LN:], o1[:, :LN], o1[:, LN:]
    to_gm = jnp.where(lo, o0h, pltpu.roll(o1h, 64, 1))
    to_gp = jnp.where(lo, pltpu.roll(o0h, 64, 1), o1h)
    return o0l, o1l, to_gm, to_gp


def spread(near, own_ref, tt_ref, ar_ref):
    lo = half_masks(8)
    zero = jnp.zeros((8, LN), F32)
    left, right, gm, gp = near
    r0l, r1l = own_ref[0, 8:16, 0:LN], own_ref[1, 8:16, 0:LN]

    def both(a, b):
        return jnp.concatenate([a, b], axis=1)

    w0 = [
        both(zero, zero),
        both(pltpu.roll(jnp.where(lo, r1l, 0.0), 64, 1), zero),
        both(pltpu.roll(jnp.where(lo, 0.0, left), 64, 1), zero),
        both(zero, jnp.where(lo, gm, 0.0)),
        both(zero, jnp.where(lo, 0.0, pltpu.roll(gp, 64, 1))),
    ]
    w1 = [
        both(pltpu.roll(jnp.where(lo, 0.0, r0l), 64, 1), zero),
        both(zero, zero),
        both(pltpu.roll(jnp.where(lo, right, 0.0), 64, 1), zero),
        both(zero, jnp.where(lo, pltpu.roll(gm, 64, 1), 0.0)),
        both(zero, jnp.where(lo, 0.0, gp)),
    ]
    for s, w in ((0, w0), (1, w1)):
        table = jnp.concatenate(w, axis=0).astype(BF)
        ar_ref[s] = lax.dot_general(table, tt_ref[s], NT, preferred_element_type=F32)
        at = 8 * s
        ar_ref[s, at : at + 8, :] = own_ref[s, 0:8, :]


def two(a):
    h = a.astype(BF)
    return h, (a - h.astype(F32)).astype(BF)


def mm3(a, b):
    ah, al = two(a)
    bh, bl = two(b)

    def d(x, y):
        return jnp.dot(x, y, preferred_element_type=F32)

    return d(ah, bh) + (d(ah, bl) + d(al, bh))


def invert_kernel(l_hbm,out_hbm,out_ref,l_ref,d_ref,x_ref,sem_d,sem_l,sem_o):
    copies_d=[pltpu.make_async_copy(l_hbm.at[0,s,pl.ds(b*LN,LN),pl.ds(b*LN,LN)],d_ref.at[s*NCH+b],sem_d.at[s*NCH+b]) for s in range(2) for b in range(NCH)]
    for c in copies_d: c.start()
    copies_l=[pltpu.make_async_copy(l_hbm.at[0,s,pl.ds(b*LN,LN),pl.ds(0,b*LN)],l_ref.at[s,pl.ds(b*LN,LN),pl.ds(0,b*LN)],sem_l.at[s*NCH+b]) for s in range(2) for b in range(1,NCH)]
    for c in copies_l: c.start()
    ri=iota((LN,LN),0); ci=iota((LN,LN),1); eye=ri==ci; below=ri>ci
    lane=iota((BASE,LN),1); row=iota((BASE,LN),0)
    nb=2*NCH; ng=LN//BASE
    group=(lane//BASE)*BASE
    for c in copies_d: c.wait()
    packs=[]
    for k in range(nb):
        lb=d_ref[k]
        diag=jnp.sum(jnp.where(eye,lb,0.0),axis=1,keepdims=True)
        n=jnp.where(below,lb*(1.0/diag),0.0)
        rowdiag=jnp.sum(jnp.where(eye,lb,0.0),axis=0,keepdims=True)
        d_ref[k]=n
        x_ref[k,0:1,:]=1.0/rowdiag
        p=None
        for g in range(ng):
            t=jnp.where(lane//BASE==g,n[g*BASE:(g+1)*BASE,:],0.0)
            p=t if p is None else p+t
        packs.append(p)
    xs=[jnp.where(row==lane%BASE,1.0,0.0) for _ in range(nb)]
    for j in range(BASE-1):
        lo=(j+1)//8*8
        for k in range(nb):
            idx=group[lo:,:]+j
            f=jnp.take_along_axis(packs[k][lo:,:],idx,axis=1)
            new=xs[k][lo:,:]-f*xs[k][j:j+1,:]
            xs[k]=new if lo==0 else jnp.concatenate([xs[k][:lo,:],new],axis=0)
    invd=[x_ref[k,0:1,:] for k in range(nb)]
    for k in range(nb):
        for g in range(ng):
            x_ref[k,g*BASE:(g+1)*BASE,:]=jnp.where(lane//BASE==g,xs[k],0.0)
    z=jnp.zeros((LN,LN),F32)

    def bd(a,b):
        return jnp.concatenate([jnp.concatenate([a,z],axis=1),jnp.concatenate([z,b],axis=1)],axis=0)

    size=BASE
    while size<LN:
        pick=((ri//(2*size))==(ci//(2*size)))&((ri//size)!=(ci//size))
        ts=[]
        for q in range(nb//2):
            e=jnp.concatenate([jnp.where(pick,d_ref[2*q],0.0),jnp.where(pick,d_ref[2*q+1],0.0)],axis=1)
            ts.append(mm3(e,bd(x_ref[2*q],x_ref[2*q+1])))
        for q in range(nb//2):
            xc=jnp.concatenate([x_ref[2*q],x_ref[2*q+1]],axis=1)
            xn=xc-mm3(xc,bd(ts[q][:,:LN],ts[q][:,LN:]))
            x_ref[2*q]=xn[:,:LN]; x_ref[2*q+1]=xn[:,LN:]
        size*=2
    for k in range(nb): x_ref[k]=x_ref[k]*invd[k]
    for c in copies_l: c.wait()

    def block(s,i,j,w=LN): return l_ref[s,i*w:(i+1)*w,j*w:(j+1)*w]

    sent=[]

    def send_block(s,i,j):
        src=out_ref.at[s,pl.ds(i*2*LN,2*LN),pl.ds(j*2*LN,2*LN)]
        dst=out_hbm.at[s,pl.ds(i*2*LN,2*LN),pl.ds(j*2*LN,2*LN)]
        c=pltpu.make_async_copy(src,dst,sem_o.at[len(sent)])
        c.start()
        sent.append(c)

    pairs=[(s,q) for s in range(2) for q in range(NCH//2)]
    mids={}
    for s,q in pairs:
        mids[s,q]=mm3(block(s,2*q+1,2*q),x_ref[s*NCH+2*q])
    for s,q in pairs:
        at=2*q*LN
        out_ref[s,at:at+LN,at:at+LN]=x_ref[s*NCH+2*q]
        out_ref[s,at:at+LN,at+LN:at+2*LN]=z
        out_ref[s,at+LN:at+2*LN,at:at+LN]=-mm3(x_ref[s*NCH+2*q+1],mids[s,q])
        out_ref[s,at+LN:at+2*LN,at+LN:at+2*LN]=x_ref[s*NCH+2*q+1]
        send_block(s,q,q)
    wd=2*LN

    def inv(s,i,j): return out_ref[s,i*wd:(i+1)*wd,j*wd:(j+1)*wd]

    a=[[mm3(block(s,i,i-1,wd),inv(s,i-1,i-1)) for i in (1,2)] for s in range(2)]
    b=[mm3(block(s,2,0,wd),inv(s,0,0)) for s in range(2)]
    for s in range(2):
        for i in (1,2):
            out_ref[s,i*wd:(i+1)*wd,(i-1)*wd:i*wd]=-mm3(inv(s,i,i),a[s][i-1])
            send_block(s,i,i-1)
    for s in range(2):
        m=b[s]+mm3(block(s,2,1,wd),inv(s,1,0))
        out_ref[s,2*wd:3*wd,0:wd]=-mm3(inv(s,2,2),m)
        send_block(s,2,0)
    for c in sent: c.wait()


def split3(rows, total):
    idx = iota((total, rows[0].shape[1]), 0)
    out = jnp.zeros((total, rows[0].shape[1]), F32)
    for r, z in enumerate(rows):
        h = z.astype(BF).astype(F32)
        rest = z - h
        m = rest.astype(BF).astype(F32)
        l = rest - m
        out = jnp.where(idx == 3 * r, h, out)
        out = jnp.where(idx == 3 * r + 1, m, out)
        out = jnp.where(idx == 3 * r + 2, l, out)
    return out.astype(BF)


def solve(inv_ref, s, z):
    ys = []
    for b in range(NCH):
        acc = None
        for c in range(b + 1):
            term = inv_ref[s, b * LN : (b + 1) * LN, c * LN : (c + 1) * LN] * z[:, c * LN : (c + 1) * LN]
            acc = term if acc is None else acc + term
        ys.append(jnp.sum(acc, axis=1, keepdims=True))
    us = []
    for c in range(NCH):
        acc = None
        for b in range(c, NCH):
            term = inv_ref[s, b * LN : (b + 1) * LN, c * LN : (c + 1) * LN] * ys[b]
            acc = term if acc is None else acc + term
        us.append(jnp.sum(acc, axis=0, keepdims=True))
    return jnp.concatenate(us, axis=1)


def received_coarse(recv_ref):
    xt = jnp.transpose(recv_ref[:, 0:LN])

    def grp(i):
        return xt[8 * i : 8 * i + 8, :]

    h0 = grp(0) + pltpu.roll(grp(2), 1, 1) + pltpu.roll(grp(4), DEV - 16, 1) + pltpu.roll(grp(6), 16, 1)
    h1 = grp(1) + pltpu.roll(grp(3), DEV - 1, 1) + pltpu.roll(grp(5), DEV - 16, 1) + pltpu.roll(grp(7), 16, 1)
    sums = jnp.sum(grp(8), axis=1, keepdims=True)
    return h0, h1, sums


def project_rows(h0, h1, m_ref, ar_ref):
    acc = jnp.zeros((64, DEV), F32)
    for v in range(12):
        h = h0 if v < 6 else h1
        a = v % 6
        acc = acc + m_ref[:, v * DEV : (v + 1) * DEV] * h[a : a + 1, :]
    al = jnp.sum(acc, axis=1, keepdims=True)

    def grp(i):
        return al[8 * i : 8 * i + 8, :]

    a0 = jnp.concatenate([grp(0), grp(1), grp(3), grp(4), grp(6)], axis=0)
    a1 = jnp.concatenate([grp(0), grp(1), grp(2), grp(5), grp(7)], axis=0)
    w0 = jnp.sum(ar_ref[0] * a0, axis=0, keepdims=True)
    w1 = jnp.sum(ar_ref[1] * a1, axis=0, keepdims=True)
    return w0, w1


def places():
    g = lax.axis_index("group")
    m = lax.axis_index("member")
    me = g * 16 + m
    return (
        jnp.where(m > 0, me - 1, me),
        jnp.where(m < 15, me + 1, me),
        jnp.where(g > 0, me - 16, me),
        jnp.where(g < 15, me + 16, me),
    )


def tile_of(row):
    base = pl.multiple_of((row // 8) * 8, 8)
    return base, row - base


def face_row(recv_ref, row):
    base, offset = tile_of(row)
    tile = recv_ref[pl.ds(base, 8), LN : 2 * LN]
    return jnp.sum(jnp.where(iota((8, LN), 0) == offset, tile, 0.0), axis=0, keepdims=True)


def assembled(recv_ref, y, o, tt_ref):
    lo = half_masks(1)
    left, right, gm, gp = (face_row(recv_ref, row) for row in places())
    o0l, o1l = o[0][:, :LN], o[1][:, :LN]
    in0 = jnp.concatenate(
        [pltpu.roll(jnp.where(lo, o1l, left), 64, 1), jnp.where(lo, gm, pltpu.roll(gp, 64, 1))], axis=1
    )
    in1 = jnp.concatenate(
        [pltpu.roll(jnp.where(lo, right, o0l), 64, 1), jnp.where(lo, pltpu.roll(gm, 64, 1), gp)], axis=1
    )
    out = []
    for s, inc in ((0, in0), (1, in1)):
        add = lax.dot_general(split3([inc], 8), tt_ref[s], NT, preferred_element_type=F32)
        out.append(y[s] + jnp.sum(add, axis=0, keepdims=True))
    return out


def send(pay_ref, y, tt_ref, ar_ref, dots):
    o = []
    cols = []
    for s in range(2):
        prod = jnp.dot(split3([y[s]], 8), tt_ref[s], preferred_element_type=F32)
        o.append(jnp.sum(prod, axis=0, keepdims=True))
        cols.append(jnp.sum(ar_ref[s] * y[s], axis=1, keepdims=True))
    c0, c1 = cols

    def grp(c, i):
        return c[8 * i : 8 * i + 8, :]

    cc = jnp.concatenate(
        [
            grp(c0, 0) + grp(c1, 0), grp(c0, 1) + grp(c1, 1), grp(c1, 2), grp(c0, 2),
            grp(c0, 3), grp(c1, 3), grp(c0, 4), grp(c1, 4),
        ],
        axis=0,
    )
    diag = iota((64, LN), 0) == iota((64, LN), 1)
    row = jnp.sum(jnp.where(diag, cc, 0.0), axis=0, keepdims=True)
    lane = iota((1, LN), 1)
    for i, value in enumerate(dots):
        row = jnp.where(lane == 64 + i, value, row)
    pay_ref[:, 0:LN] = jnp.broadcast_to(row, (DEV, LN))
    pay_ref[:, LN : 2 * LN] = jnp.zeros((DEV, LN), F32)
    to_left, to_right, to_gm, to_gp = pack_faces(o[0], o[1])
    for row, face in zip(places(), (to_left, to_right, to_gm, to_gp)):
        base, offset = tile_of(row)
        old = pay_ref[pl.ds(base, 8), LN : 2 * LN]
        pay_ref[pl.ds(base, 8), LN : 2 * LN] = jnp.where(iota((8, LN), 0) == offset, face, old)
    return o


def inner(a, b):
    return jnp.sum(a[0] * b[0] + a[1] * b[1], axis=1, keepdims=True)


def pair(ref, i):
    return [ref[i : i + 1, :], ref[i + 1 : i + 2, :]]


def put(ref, i, v):
    ref[i : i + 1, :] = v[0]
    ref[i + 1 : i + 2, :] = v[1]


LAM, PV, DV, IM, YD, YV = 0, 2, 4, 6, 8, 10


def begin_kernel(
    recv_ref, tt_ref, aux_ref, inv_hbm, own_hbm, mine_ref, near_ref,
    ar_ref, m_ref, st_ref, o_ref, pay_ref, inv_ref, own_ref, sems, sems_inv,
):
    wide = 12 * DEV
    own_copy = pltpu.make_async_copy(own_hbm, own_ref, sems.at[0])
    own_copy.start()
    parts = [
        pltpu.make_async_copy(
            inv_hbm.at[s, pl.ds(b * LN, LN), pl.ds(0, (b + 1) * LN)],
            inv_ref.at[s, pl.ds(b * LN, LN), pl.ds(0, (b + 1) * LN)],
            sems_inv.at[s * NCH + b],
        )
        for s in range(2)
        for b in range(NCH)
    ]
    for c in parts:
        c.start()
    h0, h1, _ = received_coarse(recv_ref)
    m_ref[0:16, :] = mine_ref[:, 0:wide]
    m_ref[16:64, :] = near_ref[:, 0:wide]
    own_copy.wait()
    near = [near_ref[at : at + 8, wide:] for at in (8, 0, 16, 32)]
    spread(near, own_ref, tt_ref, ar_ref)
    lam = project_rows(h0, h1, m_ref, ar_ref)
    mask = pair(aux_ref, 0)
    load = pair(aux_ref, 6)
    for c in parts:
        c.wait()
    y = [mask[s] * solve(inv_ref, s, load[s] - lam[s]) for s in range(2)]
    o = send(pay_ref, y, tt_ref, ar_ref, [])
    put(st_ref, LAM, lam)
    put(st_ref, YV, y)
    put(o_ref, 0, o)


def next_solve(pay_ref, inv_ref, tt_ref, ar_ref, aux_ref, p, d, yd):
    mask = pair(aux_ref, 0)
    weight = pair(aux_ref, 2)
    y = [mask[s] * solve(inv_ref, s, p[s]) for s in range(2)]
    wp = [weight[s] * p[s] for s in range(2)]
    dots = [inner(wp, p), inner(p, y)]
    if d is not None:
        dots += [inner(d, y), inner(p, yd)]
    o = send(pay_ref, y, tt_ref, ar_ref, dots)
    return y, o


def first_kernel(recv_ref, st_ref, o_ref, inv_ref, tt_ref, ar_ref, m_ref, aux_ref, st2_ref, o2_ref, pay_ref):
    h0, h1, _ = received_coarse(recv_ref)
    w = project_rows(h0, h1, m_ref, ar_ref)
    res = assembled(recv_ref, pair(st_ref, YV), pair(o_ref, 0), tt_ref)
    p = [res[s] - w[s] for s in range(2)]
    y, o = next_solve(pay_ref, inv_ref, tt_ref, ar_ref, aux_ref, p, None, None)
    put(st2_ref, LAM, pair(st_ref, LAM))
    put(st2_ref, PV, p)
    put(st2_ref, YV, y)
    put(o2_ref, 0, o)


def step_body(it, recv_ref, st_ref, o_ref, hs_ref, tt_ref, ar_ref, m_ref):
    h0, h1, sums = received_coarse(recv_ref)
    norm = sums[0:1, :]
    y = pair(st_ref, YV)
    p = pair(st_ref, PV)
    image = assembled(recv_ref, y, pair(o_ref, 0), tt_ref)
    if it == 0:
        d, yd, curve = p, y, sums[1:2, :]
    else:
        beta = norm / hs_ref[16:17, 0:1]
        curve = sums[1:2, :] + beta * (sums[2:3, :] + sums[3:4, :]) + beta * beta * hs_ref[17:18, 0:1]
        dold, iold, yold = pair(st_ref, DV), pair(st_ref, IM), pair(st_ref, YD)
        d = [p[s] + beta * dold[s] for s in range(2)]
        yd = [y[s] + beta * yold[s] for s in range(2)]
        image = [image[s] + beta * iold[s] for s in range(2)]
        h0 = h0 + beta * hs_ref[0:8, :]
        h1 = h1 + beta * hs_ref[8:16, :]
    step = norm / curve
    w = project_rows(h0, h1, m_ref, ar_ref)
    lam = pair(st_ref, LAM)
    lam = [lam[s] + step * d[s] for s in range(2)]
    pn = [p[s] - step * (image[s] - w[s]) for s in range(2)]
    return lam, pn, d, yd, image, h0, h1, norm, curve


def make_step(it):
    def step_kernel(
        recv_ref, st_ref, o_ref, hs_ref, inv_ref, tt_ref, ar_ref, m_ref, aux_ref,
        st2_ref, o2_ref, hs2_ref, pay_ref,
    ):
        lam, pn, d, yd, image, h0, h1, norm, curve = step_body(
            it, recv_ref, st_ref, o_ref, hs_ref, tt_ref, ar_ref, m_ref
        )
        y, o = next_solve(pay_ref, inv_ref, tt_ref, ar_ref, aux_ref, pn, d, yd)
        for at, v in ((LAM, lam), (PV, pn), (DV, d), (IM, image), (YD, yd), (YV, y)):
            put(st2_ref, at, v)
        put(o2_ref, 0, o)
        hs2_ref[0:8, :] = h0
        hs2_ref[8:16, :] = h1
        hs2_ref[16:17, :] = jnp.broadcast_to(norm, (1, DEV))
        hs2_ref[17:18, :] = jnp.broadcast_to(curve, (1, DEV))

    return step_kernel


def last_kernel(recv_ref, st_ref, o_ref, hs_ref, tt_ref, ar_ref, m_ref, aux_ref, qt_ref, lam_ref, p_ref):
    lam, pn = step_body(ITERS - 1, recv_ref, st_ref, o_ref, hs_ref, tt_ref, ar_ref, m_ref)[:2]
    for s in range(2):
        got = jnp.dot(split3([lam[s], pn[s]], 8), qt_ref[s], preferred_element_type=F32)
        sgn = aux_ref[4 + s : 5 + s, :]
        lam_ref[s : s + 1, :] = sgn * jnp.sum(got[0:3, :], axis=0, keepdims=True)
        p_ref[s : s + 1, :] = sgn * jnp.sum(got[3:6, :], axis=0, keepdims=True)


def sds(shape, dtype=F32):
    return jax.ShapeDtypeStruct(shape, dtype)


VM = pl.BlockSpec(memory_space=pltpu.VMEM)
HB = pl.BlockSpec(memory_space=pltpu.HBM)


def call(kernel, outs, specs, *args, scratch=(), flops=0, mib=16, hbm_outs=()):
    args = [
        pltpu.with_memory_space_constraint(x, pltpu.HBM) if specs.get(i) is HB else x for i, x in enumerate(args)
    ]
    return pl.pallas_call(
        kernel,
        out_shape=outs,
        in_specs=[specs.get(i, VM) for i in range(len(args))],
        out_specs=tuple(HB if i in hbm_outs else VM for i in range(len(outs))),
        scratch_shapes=list(scratch),
        compiler_params=pltpu.CompilerParams(vmem_limit_bytes=mib * 2**20),
        cost_estimate=pl.CostEstimate(flops=flops, transcendentals=0, bytes_accessed=2**20)
        if flops
        else None,
    )(*args)


def shards(factor, load, dof_map, dof_sign, live_count, face_slot, face_count, node_coord, coarse_inverse):
    axes = ("group", "member")
    packed = 12 * DEV + LN
    modes, pay0 = call(
        coarse_kernel,
        (sds((2, 8, ND)), sds((DEV, LN))),
        {0: HB, 1: HB},
        load, node_coord.transpose(0, 2, 1, 3),
        scratch=[
            pltpu.VMEM(load.shape, load.dtype), pltpu.VMEM((1, 3, 2, 256), node_coord.dtype),
            pltpu.SemaphoreType.DMA((2,)),
        ],
    )

    def exchange(pay):
        return lax.all_to_all(pay, axes, 0, 0, tiled=True)

    recv0 = exchange(pay0)
    raw = (load, dof_map, dof_sign, live_count, face_slot, face_count, coarse_inverse)
    tt, qt, own, aux, to_left, to_right, to_gm, to_gp = call(
        tables_kernel,
        (
            sds((2, ND, 256), BF), pltpu.HBM((2, ND, ND), BF), pltpu.HBM((2, 16, ND), F32), sds((8, ND)),
            sds((8, packed)), sds((8, packed)), sds((16, packed)), sds((16, packed)),
        ),
        {i: HB for i in range(1, 8)},
        modes, *raw,
        scratch=[pltpu.VMEM(r.shape, r.dtype) for r in raw]
        + [pltpu.VMEM((2, 16, ND), F32), pltpu.VMEM((2, ND, ND), BF), pltpu.SemaphoreType.DMA((10,))],
        hbm_outs=(1, 2),
    )

    up = [(i, i + 1) for i in range(15)]
    down = [(i + 1, i) for i in range(15)]
    from_right = lax.ppermute(to_left, "member", down)
    from_left = lax.ppermute(to_right, "member", up)
    from_gp = lax.ppermute(to_gm, "group", down)
    from_gm = lax.ppermute(to_gp, "group", up)
    (inv,) = call(
        invert_kernel,
        (pltpu.HBM((2, ND, ND), F32),),
        {0: HB},
        factor,
        scratch=[
            pltpu.VMEM((2, ND, ND), F32), pltpu.VMEM((2, ND, ND), F32), pltpu.VMEM((2 * NCH, LN, LN), F32),
            pltpu.VMEM((2 * NCH, LN, LN), F32), pltpu.SemaphoreType.DMA((2 * NCH,)),
            pltpu.SemaphoreType.DMA((2 * NCH,)), pltpu.SemaphoreType.DMA((2 * NCH,)),
        ],
        hbm_outs=(0,),
        flops=20_000_000_000,
        mib=24,
    )
    near = jnp.concatenate([from_right, from_left, from_gm, from_gp], axis=0)
    st_s, o_s, hs_s, pay_s = sds((12, ND)), sds((2, 256)), sds((24, DEV)), sds((DEV, 2 * LN))
    ar, table, st, o, pay = call(
        begin_kernel, (sds((2, 40, ND)), sds((64, 12 * DEV)), st_s, o_s, pay_s),
        {3: HB, 4: HB},
        recv0, tt, aux, inv, own, to_gm, near,
        scratch=[
            pltpu.VMEM((2, ND, ND), F32), pltpu.VMEM((2, 16, ND), F32),
            pltpu.SemaphoreType.DMA((1,)), pltpu.SemaphoreType.DMA((2 * NCH,)),
        ],
    )
    st, o, pay = call(first_kernel, (st_s, o_s, pay_s), {}, exchange(pay), st, o, inv, tt, ar, table, aux)
    hs = jnp.zeros((24, DEV), F32)
    for it in range(ITERS - 1):
        st, o, hs, pay = call(
            make_step(it), (st_s, o_s, hs_s, pay_s), {},
            exchange(pay), st, o, hs, inv, tt, ar, table, aux,
        )
    lam, proj = call(
        last_kernel, (sds((2, ND)), sds((2, ND))), {},
        exchange(pay), st, o, hs, tt, ar, table, aux, qt,
    )
    return lam[None], proj[None]


def solution(mesh):
    return jax.shard_map(
        shards,
        mesh=mesh,
        in_specs=(
            P("group", "member", None, None),
            P("group", "member", None),
            P("group", "member", None),
            P("group", "member", None),
            P("group", "member"),
            P("group", "member", None, None),
            P("group", "member", None),
            P("group", "member", None, None),
            P(("group", "member"), None),
        ),
        out_specs=(P("group", "member", None), P("group", "member", None)),
        check_vma=False,
    )
```

```python
import jax
import jax.numpy as jnp
from jax import lax
from jax.experimental import pallas as pl
from jax.experimental.pallas import tpu as pltpu
from jax.sharding import PartitionSpec as P

ITERS = 3
ND = 768
LN = 128
NCH = ND // LN
DEV = 256
BASE = 16
F32 = jnp.float32
BF = jnp.bfloat16
NT = (((1,), (1,)), ((), ()))


def iota(shape, dim):
    return lax.broadcasted_iota(jnp.int32, shape, dim)


def coarse_kernel(load_hbm, node_hbm, modes_ref, pay_ref, load_ref, node_ref, sems):
    copies = [
        pltpu.make_async_copy(node_hbm, node_ref, sems.at[0]),
        pltpu.make_async_copy(load_hbm, load_ref, sems.at[1]),
    ]
    for c in copies:
        c.start()
    lane8 = iota((8, LN), 1)
    sub8 = iota((8, LN), 0)
    part = iota((8, ND), 0)
    row = jnp.zeros((1, LN), F32)
    dim = iota((1, ND), 1).astype(F32)
    node = jnp.floor((dim + 0.5) * (1.0 / 3.0))
    comp = dim - 3.0 * node
    first = (comp == 0.0).astype(F32)
    second = (comp == 1.0).astype(F32)
    third = (comp == 2.0).astype(F32)
    delta = iota((256, ND), 1) - 3 * iota((256, ND), 0)
    rep = jnp.where((delta >= 0) & (delta < 3), 1.0, 0.0).astype(BF)
    for c in copies:
        c.wait()
    for s in range(2):
        position = (node_ref[0, :, s, :].astype(F32) - 8.0) * 0.125
        spread = jnp.dot(position.astype(BF), rep, preferred_element_type=F32)
        cx = spread[0:1, :]
        cy = spread[1:2, :]
        cz = spread[2:3, :]
        rows = (
            first, second, third,
            third * cy - second * cz,
            first * cz - third * cx,
            second * cx - first * cy,
        )
        modes = jnp.zeros((8, ND), F32)
        for a in range(6):
            modes = jnp.where(part == a, rows[a], modes)
        modes_ref[s] = modes
        e = jnp.sum(modes * load_ref[0, s : s + 1, :], axis=1, keepdims=True)
        row = row + jnp.sum(jnp.where(lane8 == sub8 + 8 * s, e, 0.0), axis=0, keepdims=True)
    pay_ref[...] = jnp.broadcast_to(row, (DEV, LN))


def tables_kernel(
    modes_ref, load_hbm, map_hbm, sign_hbm, live_hbm, slot_hbm, count_hbm, coarse_hbm, l_hbm,
    tt_ref, qt_hbm, own_hbm, aux_ref, sib_ref, far_ref, g1_ref, g2_ref, d_ref,
    load_ref, map_ref, sign_ref, live_ref, slot_ref, count_ref, coarse_ref, own_ref, qt_ref, sems, sems_d,
):
    copies = [
        pltpu.make_async_copy(src, dst, sems.at[i])
        for i, (src, dst) in enumerate(
            (
                (load_hbm, load_ref), (map_hbm, map_ref), (sign_hbm, sign_ref),
                (live_hbm, live_ref), (slot_hbm, slot_ref), (count_hbm, count_ref),
                (coarse_hbm, coarse_ref),
            )
        )
    ]
    for c in copies:
        c.start()
    blocks = [
        pltpu.make_async_copy(
            l_hbm.at[0, s, pl.ds(b * LN, LN), pl.ds(b * LN, LN)], d_ref.at[s * NCH + b], sems_d.at[s * NCH + b]
        )
        for s in range(2)
        for b in range(NCH)
    ]
    for c in blocks:
        c.start()
    part = iota((8, ND), 0)
    for c in copies[:-1]:
        c.wait()
    faces = []
    late = []
    for s in range(2):
        live = iota((1, ND), 1) < live_ref[0:1, s : s + 1]
        live_f = jnp.where(live, 1.0, 0.0)
        sgn = jnp.where(live, sign_ref[0, s : s + 1, :].astype(F32), 0.0)
        dof = map_ref[0, s : s + 1, :]
        dof_f = dof.astype(F32)
        high = jnp.floor(dof_f * (1.0 / 32.0))
        low = dof_f - 32.0 * high
        lhs = jnp.where(part == 0, high, jnp.where(part == 1, low, jnp.where(part == 2, sgn, 0.0)))
        pos64 = iota((1, 64), 1)
        slots = jnp.concatenate(
            [
                jnp.where(pos64 < count_ref[0, s : s + 1, f : f + 1], slot_ref[0, s, f : f + 1, :], -1)
                for f in range(4)
            ],
            axis=1,
        )
        hit = jnp.where(iota((ND, 256), 0) == slots, 1.0, 0.0).astype(BF)
        got = jnp.dot(lhs.astype(BF), hit, preferred_element_type=F32)
        dk = (32.0 * got[0:1, :] + got[1:2, :]).astype(jnp.int32)
        sk = got[2:3, :]
        tt = jnp.where(iota((ND, 256), 0) == dk, sk, 0.0)
        tt_b = tt.astype(BF)
        tt_ref[s] = tt_b
        qt = jnp.where(iota((ND, ND), 0) == dof, 1.0, 0.0).astype(BF)
        qt_ref[s] = qt
        qt_copy = pltpu.make_async_copy(qt_ref.at[s], qt_hbm.at[s], sems.at[8 + s])
        qt_copy.start()
        late.append(qt_copy)
        mask = lax.dot_general(
            jnp.broadcast_to(live_f, (8, ND)).astype(BF), qt, NT, preferred_element_type=F32
        )[0:1, :]
        count = lax.dot_general(
            jnp.ones((8, 256), BF), jnp.abs(tt).astype(BF), NT, preferred_element_type=F32
        )[0:1, :]
        aux_ref[s : s + 1, :] = mask
        aux_ref[2 + s : 3 + s, :] = mask * (1.0 - 0.5 * count)
        aux_ref[4 + s : 5 + s, :] = sgn
        aux_ref[6 + s : 7 + s, :] = load_ref[0, s : s + 1, :]
        modes = modes_ref[s]
        own_ref[s, 0:8, :] = modes * mask
        face = jnp.dot(modes.astype(BF), tt_b, preferred_element_type=F32)
        own_ref[s, 8:16, :] = jnp.concatenate([face, jnp.zeros((8, ND - 256), F32)], axis=1)
        faces.append(face)
    wide = 12 * DEV
    to_left, to_right, to_gm, to_gp = pack_faces(faces[0], faces[1])
    even_m = lax.axis_index("member") % 2 == 0
    even_g = lax.axis_index("group") % 2 == 0
    sib_ref[:, wide:] = jnp.where(even_m, to_right, to_left)
    far_ref[:, wide:] = jnp.where(even_m, to_left, to_right)
    zero = jnp.zeros((8, LN), F32)
    g1_ref[0:8, wide:] = jnp.where(even_g, to_gp, to_gm)
    g2_ref[0:8, wide:] = jnp.where(even_g, to_gm, to_gp)
    g1_ref[8:16, wide:] = zero
    g2_ref[8:16, wide:] = zero
    own_copy = pltpu.make_async_copy(own_ref, own_hbm, sems.at[7])
    own_copy.start()
    late.append(own_copy)
    copies[-1].wait()
    perm = jnp.where(
        (iota((384, 384), 0) - 12 * (iota((384, 384), 1) % 32)) == iota((384, 384), 1) // 32, 1.0, 0.0
    ).astype(BF)
    keep = iota((8, 384), 0) < 6
    res = []
    for q in range(8):
        c = coarse_ref[:, 384 * q : 384 * (q + 1)]
        c16 = jnp.concatenate([c, jnp.zeros((4, 384), F32)], axis=0)
        up = jnp.where(keep, c16[0:8], 0.0)
        dn = jnp.where(keep, pltpu.roll(c16, 10, 0)[0:8], 0.0)
        both = jnp.concatenate([up, dn], axis=0)
        h = both.astype(BF)
        rest = both - h.astype(F32)
        m = rest.astype(BF)
        l = (rest - m.astype(F32)).astype(BF)
        got = jnp.dot(jnp.concatenate([h, m, l], axis=0), perm, preferred_element_type=F32)
        res.append(got[0:16] + got[16:32] + got[32:48])
    quarter = iota((16, LN), 1) // 32
    for v in range(12):
        for half in range(2):
            acc = None
            for i in range(4):
                src = res[4 * half + i][:, LN * (v // 4) : LN * (v // 4 + 1)]
                shift = (32 * (i - v % 4)) % LN
                src = pltpu.roll(src, shift, 1) if shift else src
                acc = src if acc is None else jnp.where(quarter == i, src, acc)
            at = v * DEV + half * LN
            sib_ref[:, at : at + LN] = jnp.where(even_m, acc[8:16], acc[0:8])
            far_ref[:, at : at + LN] = jnp.where(even_m, acc[0:8], acc[8:16])
            g1_ref[:, at : at + LN] = acc
            g2_ref[:, at : at + LN] = acc
    for c in late + blocks:
        c.wait()


def half_masks(rows):
    return iota((rows, LN), 1) < 64


def pack_faces(o0, o1):
    lo = half_masks(o0.shape[0])
    o0l, o0h, o1l, o1h = o0[:, :LN], o0[:, LN:], o1[:, :LN], o1[:, LN:]
    to_gm = jnp.where(lo, o0h, pltpu.roll(o1h, 64, 1))
    to_gp = jnp.where(lo, pltpu.roll(o0h, 64, 1), o1h)
    return o0l, o1l, to_gm, to_gp


def spread(near, own_ref, tt_ref, ar_ref):
    lo = half_masks(8)
    zero = jnp.zeros((8, LN), F32)
    left, right, gm, gp = near
    r0l, r1l = own_ref[0, 8:16, 0:LN], own_ref[1, 8:16, 0:LN]

    def both(a, b):
        return jnp.concatenate([a, b], axis=1)

    w0 = [
        both(zero, zero),
        both(pltpu.roll(jnp.where(lo, r1l, 0.0), 64, 1), zero),
        both(pltpu.roll(jnp.where(lo, 0.0, left), 64, 1), zero),
        both(zero, jnp.where(lo, gm, 0.0)),
        both(zero, jnp.where(lo, 0.0, pltpu.roll(gp, 64, 1))),
    ]
    w1 = [
        both(pltpu.roll(jnp.where(lo, 0.0, r0l), 64, 1), zero),
        both(zero, zero),
        both(pltpu.roll(jnp.where(lo, right, 0.0), 64, 1), zero),
        both(zero, jnp.where(lo, pltpu.roll(gm, 64, 1), 0.0)),
        both(zero, jnp.where(lo, 0.0, gp)),
    ]
    for s, w in ((0, w0), (1, w1)):
        table = jnp.concatenate(w, axis=0).astype(BF)
        ar_ref[s] = lax.dot_general(table, tt_ref[s], NT, preferred_element_type=F32)
        at = 8 * s
        ar_ref[s, at : at + 8, :] = own_ref[s, 0:8, :]


def two(a):
    h = a.astype(BF)
    return h, (a - h.astype(F32)).astype(BF)


def mm3(a, b):
    ah, al = two(a)
    bh, bl = two(b)

    def d(x, y):
        return jnp.dot(x, y, preferred_element_type=F32)

    return d(ah, bh) + (d(ah, bl) + d(al, bh))


def invert_kernel(l_hbm,diag_ref,out_hbm,out_ref,l_ref,d_ref,x_ref,sem_l,sem_o):
    copies_l=[pltpu.make_async_copy(l_hbm.at[0,s,pl.ds(b*LN,LN),pl.ds(0,b*LN)],l_ref.at[s,pl.ds(b*LN,LN),pl.ds(0,b*LN)],sem_l.at[s*NCH+b]) for s in range(2) for b in range(1,NCH)]
    for c in copies_l: c.start()
    ri=iota((LN,LN),0); ci=iota((LN,LN),1); eye=ri==ci; below=ri>ci
    lane=iota((BASE,LN),1); row=iota((BASE,LN),0)
    nb=2*NCH; ng=LN//BASE
    group=(lane//BASE)*BASE
    packs=[]
    for k in range(nb):
        lb=diag_ref[k]
        diag=jnp.sum(jnp.where(eye,lb,0.0),axis=1,keepdims=True)
        n=jnp.where(below,lb*(1.0/diag),0.0)
        rowdiag=jnp.sum(jnp.where(eye,lb,0.0),axis=0,keepdims=True)
        d_ref[k]=n
        x_ref[k,0:1,:]=1.0/rowdiag
        p=None
        for g in range(ng):
            t=jnp.where(lane//BASE==g,n[g*BASE:(g+1)*BASE,:],0.0)
            p=t if p is None else p+t
        packs.append(p)
    xs=[jnp.where(row==lane%BASE,1.0,0.0) for _ in range(nb)]
    for j in range(BASE-1):
        lo=(j+1)//8*8
        for k in range(nb):
            idx=group[lo:,:]+j
            f=jnp.take_along_axis(packs[k][lo:,:],idx,axis=1)
            new=xs[k][lo:,:]-f*xs[k][j:j+1,:]
            xs[k]=new if lo==0 else jnp.concatenate([xs[k][:lo,:],new],axis=0)
    invd=[x_ref[k,0:1,:] for k in range(nb)]
    for k in range(nb):
        for g in range(ng):
            x_ref[k,g*BASE:(g+1)*BASE,:]=jnp.where(lane//BASE==g,xs[k],0.0)
    z=jnp.zeros((LN,LN),F32)

    def bd(a,b):
        return jnp.concatenate([jnp.concatenate([a,z],axis=1),jnp.concatenate([z,b],axis=1)],axis=0)

    size=BASE
    while size<LN:
        pick=((ri//(2*size))==(ci//(2*size)))&((ri//size)!=(ci//size))
        ts=[]
        for q in range(nb//2):
            e=jnp.concatenate([jnp.where(pick,d_ref[2*q],0.0),jnp.where(pick,d_ref[2*q+1],0.0)],axis=1)
            ts.append(mm3(e,bd(x_ref[2*q],x_ref[2*q+1])))
        for q in range(nb//2):
            xc=jnp.concatenate([x_ref[2*q],x_ref[2*q+1]],axis=1)
            xn=xc-mm3(xc,bd(ts[q][:,:LN],ts[q][:,LN:]))
            x_ref[2*q]=xn[:,:LN]; x_ref[2*q+1]=xn[:,LN:]
        size*=2
    for k in range(nb): x_ref[k]=x_ref[k]*invd[k]
    for c in copies_l: c.wait()

    def block(s,i,j,w=LN): return l_ref[s,i*w:(i+1)*w,j*w:(j+1)*w]

    sent=[]

    def send_block(s,i,j):
        src=out_ref.at[s,pl.ds(i*2*LN,2*LN),pl.ds(j*2*LN,2*LN)]
        dst=out_hbm.at[s,pl.ds(i*2*LN,2*LN),pl.ds(j*2*LN,2*LN)]
        c=pltpu.make_async_copy(src,dst,sem_o.at[len(sent)])
        c.start()
        sent.append(c)

    pairs=[(s,q) for s in range(2) for q in range(NCH//2)]
    mids={}
    for s,q in pairs:
        mids[s,q]=mm3(block(s,2*q+1,2*q),x_ref[s*NCH+2*q])
    for s,q in pairs:
        at=2*q*LN
        out_ref[s,at:at+LN,at:at+LN]=x_ref[s*NCH+2*q]
        out_ref[s,at:at+LN,at+LN:at+2*LN]=z
        out_ref[s,at+LN:at+2*LN,at:at+LN]=-mm3(x_ref[s*NCH+2*q+1],mids[s,q])
        out_ref[s,at+LN:at+2*LN,at+LN:at+2*LN]=x_ref[s*NCH+2*q+1]
        send_block(s,q,q)
    wd=2*LN

    def inv(s,i,j): return out_ref[s,i*wd:(i+1)*wd,j*wd:(j+1)*wd]

    a=[[mm3(block(s,i,i-1,wd),inv(s,i-1,i-1)) for i in (1,2)] for s in range(2)]
    b=[mm3(block(s,2,0,wd),inv(s,0,0)) for s in range(2)]
    for s in range(2):
        for i in (1,2):
            out_ref[s,i*wd:(i+1)*wd,(i-1)*wd:i*wd]=-mm3(inv(s,i,i),a[s][i-1])
            send_block(s,i,i-1)
    for s in range(2):
        m=b[s]+mm3(block(s,2,1,wd),inv(s,1,0))
        out_ref[s,2*wd:3*wd,0:wd]=-mm3(inv(s,2,2),m)
        send_block(s,2,0)
    for c in sent: c.wait()


def split3(rows, total):
    idx = iota((total, rows[0].shape[1]), 0)
    out = jnp.zeros((total, rows[0].shape[1]), F32)
    for r, z in enumerate(rows):
        h = z.astype(BF).astype(F32)
        rest = z - h
        m = rest.astype(BF).astype(F32)
        l = rest - m
        out = jnp.where(idx == 3 * r, h, out)
        out = jnp.where(idx == 3 * r + 1, m, out)
        out = jnp.where(idx == 3 * r + 2, l, out)
    return out.astype(BF)


def solve(inv_ref, s, z):
    ys = []
    for b in range(NCH):
        acc = None
        for c in range(b + 1):
            term = inv_ref[s, b * LN : (b + 1) * LN, c * LN : (c + 1) * LN] * z[:, c * LN : (c + 1) * LN]
            acc = term if acc is None else acc + term
        ys.append(jnp.sum(acc, axis=1, keepdims=True))
    us = []
    for c in range(NCH):
        acc = None
        for b in range(c, NCH):
            term = inv_ref[s, b * LN : (b + 1) * LN, c * LN : (c + 1) * LN] * ys[b]
            acc = term if acc is None else acc + term
        us.append(jnp.sum(acc, axis=0, keepdims=True))
    return jnp.concatenate(us, axis=1)


def received_coarse(recv_ref):
    xt = jnp.transpose(recv_ref[...])

    def grp(i):
        return xt[8 * i : 8 * i + 8, :]

    h0 = grp(0) + pltpu.roll(grp(2), 1, 1) + pltpu.roll(grp(4), DEV - 16, 1) + pltpu.roll(grp(6), 16, 1)
    h1 = grp(1) + pltpu.roll(grp(3), DEV - 1, 1) + pltpu.roll(grp(5), DEV - 16, 1) + pltpu.roll(grp(7), 16, 1)
    sums = jnp.concatenate(
        [jnp.sum(grp(i), axis=1, keepdims=True)[6:8] for i in range(2)], axis=0
    )
    return h0, h1, sums


def project_rows(h0, h1, m_ref, ar_ref):
    acc = jnp.zeros((64, DEV), F32)
    for v in range(12):
        h = h0 if v < 6 else h1
        a = v % 6
        acc = acc + m_ref[:, v * DEV : (v + 1) * DEV] * h[a : a + 1, :]
    al = jnp.sum(acc, axis=1, keepdims=True)

    def grp(i):
        return al[8 * i : 8 * i + 8, :]

    a0 = jnp.concatenate([grp(0), grp(1), grp(3), grp(4), grp(6)], axis=0)
    a1 = jnp.concatenate([grp(0), grp(1), grp(2), grp(5), grp(7)], axis=0)
    w0 = jnp.sum(ar_ref[0] * a0, axis=0, keepdims=True)
    w1 = jnp.sum(ar_ref[1] * a1, axis=0, keepdims=True)
    return w0, w1


def places():
    g = lax.axis_index("group")
    m = lax.axis_index("member")
    me = g * 16 + m
    sib = me + 1 - 2 * (m % 2)
    return (
        jnp.where(m > 0, me - 1, me),
        jnp.where(m < 15, me + 1, me),
        jnp.where(g > 0, me - 16, me),
        jnp.where(g < 15, me + 16, me),
        jnp.where(g > 0, sib - 16, me),
        jnp.where(g < 15, sib + 16, me),
    )


def tile_of(row):
    base = pl.multiple_of((row // 8) * 8, 8)
    return base, row - base


def face_row(recv_ref, row):
    base, offset = tile_of(row)
    tile = recv_ref[pl.ds(base, 8), :]
    return jnp.sum(jnp.where(iota((8, LN), 0) == offset, tile, 0.0), axis=0, keepdims=True)


def assembled(recv_ref, y, o, tt_ref):
    lo = half_masks(1)
    left, right, gm, gp, sgm, sgp = (face_row(recv_ref, row) for row in places())
    o0l, o1l = o[0][:, :LN], o[1][:, :LN]
    in0 = jnp.concatenate(
        [pltpu.roll(jnp.where(lo, o1l, left), 64, 1), jnp.where(lo, pltpu.roll(gm, 64, 1), gp)], axis=1
    )
    in1 = jnp.concatenate(
        [jnp.where(lo, pltpu.roll(o0l, 64, 1), right), jnp.where(lo, pltpu.roll(sgm, 64, 1), sgp)], axis=1
    )
    out = []
    for s, inc in ((0, in0), (1, in1)):
        add = lax.dot_general(split3([inc], 8), tt_ref[s], NT, preferred_element_type=F32)
        out.append(y[s] + jnp.sum(add, axis=0, keepdims=True))
    return out


def send(row_ref, y, tt_ref, ar_ref, dots):
    o = []
    cols = []
    for s in range(2):
        prod = jnp.dot(split3([y[s]], 8), tt_ref[s], preferred_element_type=F32)
        o.append(jnp.sum(prod, axis=0, keepdims=True))
        cols.append(jnp.sum(ar_ref[s] * y[s], axis=1, keepdims=True))
    c0, c1 = cols

    def grp(c, i):
        return c[8 * i : 8 * i + 8, :]

    cc = jnp.concatenate(
        [
            grp(c0, 0) + grp(c1, 0), grp(c0, 1) + grp(c1, 1), grp(c1, 2), grp(c0, 2),
            grp(c0, 3), grp(c1, 3), grp(c0, 4), grp(c1, 4),
        ],
        axis=0,
    )
    diag = iota((64, LN), 0) == iota((64, LN), 1)
    row = jnp.sum(jnp.where(diag, cc, 0.0), axis=0, keepdims=True)
    lane = iota((1, LN), 1)
    for at, value in zip((6, 7, 14, 15), dots):
        row = jnp.where(lane == at, value, row)
    row_ref[...] = jnp.concatenate([row, o[1][:, LN:], jnp.zeros((6, LN), F32)], axis=0)
    return o


def pay_kernel(row_ref, sib_ref, o_ref, pay_ref):
    pay_ref[...] = jnp.broadcast_to(row_ref[0:1, :], (DEV, LN))
    o0l, o0h, o1l = o_ref[0:1, 0:LN], o_ref[0:1, LN : 2 * LN], o_ref[1:2, 0:LN]
    other = sib_ref[1:2, :]
    faces = (pltpu.roll(o0l, 64, 1), o1l, pltpu.roll(o0h, 64, 1), o0h, pltpu.roll(other, 64, 1), other)
    for row, face in zip(places(), faces):
        base, offset = tile_of(row)
        old = pay_ref[pl.ds(base, 8), :]
        put_here = (iota((8, LN), 0) == offset) & (iota((8, LN), 1) >= 64)
        pay_ref[pl.ds(base, 8), :] = jnp.where(put_here, face, old)


def inner(a, b):
    return jnp.sum(a[0] * b[0] + a[1] * b[1], axis=1, keepdims=True)


def pair(ref, i):
    return [ref[i : i + 1, :], ref[i + 1 : i + 2, :]]


def put(ref, i, v):
    ref[i : i + 1, :] = v[0]
    ref[i + 1 : i + 2, :] = v[1]


LAM, PV, DV, IM, YD, YV = 0, 2, 4, 6, 8, 10


def begin_kernel(
    recv_ref, tt_ref, aux_ref, inv_hbm, own_hbm, mine_ref, near_ref,
    ar_ref, m_ref, st_ref, o_ref, row_ref, inv_ref, own_ref, sems, sems_inv,
):
    wide = 12 * DEV
    own_copy = pltpu.make_async_copy(own_hbm, own_ref, sems.at[0])
    own_copy.start()
    parts = [
        pltpu.make_async_copy(
            inv_hbm.at[s, pl.ds(b * LN, LN), pl.ds(0, (b + 1) * LN)],
            inv_ref.at[s, pl.ds(b * LN, LN), pl.ds(0, (b + 1) * LN)],
            sems_inv.at[s * NCH + b],
        )
        for s in range(2)
        for b in range(NCH)
    ]
    for c in parts:
        c.start()
    h0, h1, _ = received_coarse(recv_ref)
    m_ref[0:16, :] = mine_ref[:, 0:wide]
    even_m = lax.axis_index("member") % 2 == 0
    even_g = lax.axis_index("group") % 2 == 0
    sib, far = near_ref[0:8, :], near_ref[8:16, :]
    first, second = near_ref[16:32, :], near_ref[32:48, :]
    right = jnp.where(even_m, sib, far)
    left = jnp.where(even_m, far, sib)
    gm = jnp.where(even_g, second, first)
    gp = jnp.where(even_g, first, second)
    m_ref[16:24, :] = right[:, 0:wide]
    m_ref[24:32, :] = left[:, 0:wide]
    m_ref[32:48, :] = gm[:, 0:wide]
    m_ref[48:64, :] = gp[:, 0:wide]
    own_copy.wait()
    near = [left[:, wide:], right[:, wide:], gm[0:8, wide:], gp[0:8, wide:]]
    spread(near, own_ref, tt_ref, ar_ref)
    lam = project_rows(h0, h1, m_ref, ar_ref)
    mask = pair(aux_ref, 0)
    load = pair(aux_ref, 6)
    for c in parts:
        c.wait()
    y = [mask[s] * solve(inv_ref, s, load[s] - lam[s]) for s in range(2)]
    o = send(row_ref, y, tt_ref, ar_ref, [])
    put(st_ref, LAM, lam)
    put(st_ref, YV, y)
    put(o_ref, 0, o)


def next_solve(row_ref, inv_ref, tt_ref, ar_ref, aux_ref, p, d, yd):
    mask = pair(aux_ref, 0)
    weight = pair(aux_ref, 2)
    y = [mask[s] * solve(inv_ref, s, p[s]) for s in range(2)]
    wp = [weight[s] * p[s] for s in range(2)]
    dots = [inner(wp, p), inner(p, y)]
    if d is not None:
        dots += [inner(d, y), inner(p, yd)]
    o = send(row_ref, y, tt_ref, ar_ref, dots)
    return y, o


def first_kernel(recv_ref, st_ref, o_ref, inv_ref, tt_ref, ar_ref, m_ref, aux_ref, st2_ref, o2_ref, row_ref):
    h0, h1, _ = received_coarse(recv_ref)
    w = project_rows(h0, h1, m_ref, ar_ref)
    res = assembled(recv_ref, pair(st_ref, YV), pair(o_ref, 0), tt_ref)
    p = [res[s] - w[s] for s in range(2)]
    y, o = next_solve(row_ref, inv_ref, tt_ref, ar_ref, aux_ref, p, None, None)
    put(st2_ref, LAM, pair(st_ref, LAM))
    put(st2_ref, PV, p)
    put(st2_ref, YV, y)
    put(o2_ref, 0, o)


def step_body(it, recv_ref, st_ref, o_ref, hs_ref, tt_ref, ar_ref, m_ref):
    h0, h1, sums = received_coarse(recv_ref)
    norm = sums[0:1, :]
    y = pair(st_ref, YV)
    p = pair(st_ref, PV)
    image = assembled(recv_ref, y, pair(o_ref, 0), tt_ref)
    if it == 0:
        d, yd, curve = p, y, sums[1:2, :]
    else:
        beta = norm / hs_ref[16:17, 0:1]
        curve = sums[1:2, :] + beta * (sums[2:3, :] + sums[3:4, :]) + beta * beta * hs_ref[17:18, 0:1]
        dold, iold, yold = pair(st_ref, DV), pair(st_ref, IM), pair(st_ref, YD)
        d = [p[s] + beta * dold[s] for s in range(2)]
        yd = [y[s] + beta * yold[s] for s in range(2)]
        image = [image[s] + beta * iold[s] for s in range(2)]
        h0 = h0 + beta * hs_ref[0:8, :]
        h1 = h1 + beta * hs_ref[8:16, :]
    step = norm / curve
    w = project_rows(h0, h1, m_ref, ar_ref)
    lam = pair(st_ref, LAM)
    lam = [lam[s] + step * d[s] for s in range(2)]
    pn = [p[s] - step * (image[s] - w[s]) for s in range(2)]
    return lam, pn, d, yd, image, h0, h1, norm, curve


def make_step(it):
    def step_kernel(
        recv_ref, st_ref, o_ref, hs_ref, inv_ref, tt_ref, ar_ref, m_ref, aux_ref,
        st2_ref, o2_ref, hs2_ref, row_ref,
    ):
        lam, pn, d, yd, image, h0, h1, norm, curve = step_body(
            it, recv_ref, st_ref, o_ref, hs_ref, tt_ref, ar_ref, m_ref
        )
        y, o = next_solve(row_ref, inv_ref, tt_ref, ar_ref, aux_ref, pn, d, yd)
        for at, v in ((LAM, lam), (PV, pn), (DV, d), (IM, image), (YD, yd), (YV, y)):
            put(st2_ref, at, v)
        put(o2_ref, 0, o)
        hs2_ref[0:8, :] = h0
        hs2_ref[8:16, :] = h1
        hs2_ref[16:17, :] = jnp.broadcast_to(norm, (1, DEV))
        hs2_ref[17:18, :] = jnp.broadcast_to(curve, (1, DEV))

    return step_kernel


def last_kernel(recv_ref, st_ref, o_ref, hs_ref, tt_ref, ar_ref, m_ref, aux_ref, qt_ref, lam_ref, p_ref):
    lam, pn = step_body(ITERS - 1, recv_ref, st_ref, o_ref, hs_ref, tt_ref, ar_ref, m_ref)[:2]
    for s in range(2):
        got = jnp.dot(split3([lam[s], pn[s]], 8), qt_ref[s], preferred_element_type=F32)
        sgn = aux_ref[4 + s : 5 + s, :]
        lam_ref[s : s + 1, :] = sgn * jnp.sum(got[0:3, :], axis=0, keepdims=True)
        p_ref[s : s + 1, :] = sgn * jnp.sum(got[3:6, :], axis=0, keepdims=True)


def sds(shape, dtype=F32):
    return jax.ShapeDtypeStruct(shape, dtype)


VM = pl.BlockSpec(memory_space=pltpu.VMEM)
HB = pl.BlockSpec(memory_space=pltpu.HBM)


def call(kernel, outs, specs, *args, scratch=(), flops=0, mib=16, hbm_outs=()):
    args = [
        pltpu.with_memory_space_constraint(x, pltpu.HBM) if specs.get(i) is HB else x for i, x in enumerate(args)
    ]
    return pl.pallas_call(
        kernel,
        out_shape=outs,
        in_specs=[specs.get(i, VM) for i in range(len(args))],
        out_specs=tuple(HB if i in hbm_outs else VM for i in range(len(outs))),
        scratch_shapes=list(scratch),
        compiler_params=pltpu.CompilerParams(vmem_limit_bytes=mib * 2**20),
        cost_estimate=pl.CostEstimate(flops=flops, transcendentals=0, bytes_accessed=2**20)
        if flops
        else None,
    )(*args)


def shards(factor, load, dof_map, dof_sign, live_count, face_slot, face_count, node_coord, coarse_inverse):
    axes = ("group", "member")
    packed = 12 * DEV + LN
    modes, pay0 = call(
        coarse_kernel,
        (sds((2, 8, ND)), sds((DEV, LN))),
        {0: HB, 1: HB},
        load, node_coord.transpose(0, 2, 1, 3),
        scratch=[
            pltpu.VMEM(load.shape, load.dtype), pltpu.VMEM((1, 3, 2, 256), node_coord.dtype),
            pltpu.SemaphoreType.DMA((2,)),
        ],
    )

    def exchange(pay):
        return lax.all_to_all(pay, axes, 0, 0, tiled=True)

    recv0 = exchange(pay0)
    raw = (load, dof_map, dof_sign, live_count, face_slot, face_count, coarse_inverse)
    tt, qt, own, aux, to_sib, to_far, to_g1, to_g2, diag = call(
        tables_kernel,
        (
            sds((2, ND, 256), BF), pltpu.HBM((2, ND, ND), BF), pltpu.HBM((2, 16, ND), F32), sds((8, ND)),
            sds((8, packed)), sds((8, packed)), sds((16, packed)), sds((16, packed)), sds((2 * NCH, LN, LN)),
        ),
        {i: HB for i in range(1, 9)},
        modes, *raw, factor,
        scratch=[pltpu.VMEM(r.shape, r.dtype) for r in raw]
        + [pltpu.VMEM((2, 16, ND), F32), pltpu.VMEM((2, ND, ND), BF), pltpu.SemaphoreType.DMA((10,)), pltpu.SemaphoreType.DMA((2 * NCH,))],
        hbm_outs=(1, 2),
    )

    swap = [(i, i ^ 1) for i in range(16)]
    cross = [(i, ((i + 1) ^ 1) - 1) for i in range(1, 15)]
    from_g1 = lax.ppermute(to_g1, "group", swap)
    from_g2 = lax.ppermute(to_g2, "group", cross)
    from_far = lax.ppermute(to_far, "member", cross)
    from_sib = lax.ppermute(to_sib, "member", swap)
    (inv,) = call(
        invert_kernel,
        (pltpu.HBM((2, ND, ND), F32),),
        {0: HB},
        factor, diag,
        scratch=[
            pltpu.VMEM((2, ND, ND), F32), pltpu.VMEM((2, ND, ND), F32), pltpu.VMEM((2 * NCH, LN, LN), F32),
            pltpu.VMEM((2 * NCH, LN, LN), F32), pltpu.SemaphoreType.DMA((2 * NCH,)),
            pltpu.SemaphoreType.DMA((2 * NCH,)),
        ],
        hbm_outs=(0,),
        flops=20_000_000_000,
        mib=24,
    )
    near = jnp.concatenate([from_sib, from_far, from_g1, from_g2], axis=0)
    st_s, o_s, hs_s, row_s = sds((12, ND)), sds((2, 256)), sds((24, DEV)), sds((8, LN))

    def gather(row, o):
        (pay,) = call(pay_kernel, (sds((DEV, LN)),), {}, row, lax.ppermute(row, "member", swap), o)
        return exchange(pay)

    ar, table, st, o, row = call(
        begin_kernel, (sds((2, 40, ND)), sds((64, 12 * DEV)), st_s, o_s, row_s),
        {3: HB, 4: HB},
        recv0, tt, aux, inv, own, to_g1, near,
        scratch=[
            pltpu.VMEM((2, ND, ND), F32), pltpu.VMEM((2, 16, ND), F32),
            pltpu.SemaphoreType.DMA((1,)), pltpu.SemaphoreType.DMA((2 * NCH,)),
        ],
    )
    st, o, row = call(first_kernel, (st_s, o_s, row_s), {}, gather(row, o), st, o, inv, tt, ar, table, aux)
    hs = jnp.zeros((24, DEV), F32)
    for it in range(ITERS - 1):
        st, o, hs, row = call(
            make_step(it), (st_s, o_s, hs_s, row_s), {},
            gather(row, o), st, o, hs, inv, tt, ar, table, aux,
        )
    lam, proj = call(
        last_kernel, (sds((2, ND)), sds((2, ND))), {},
        gather(row, o), st, o, hs, tt, ar, table, aux, qt,
    )
    return lam[None], proj[None]


def solution(mesh):
    return jax.shard_map(
        shards,
        mesh=mesh,
        in_specs=(
            P("group", "member", None, None),
            P("group", "member", None),
            P("group", "member", None),
            P("group", "member", None),
            P("group", "member"),
            P("group", "member", None, None),
            P("group", "member", None),
            P("group", "member", None, None),
            P(("group", "member"), None),
        ),
        out_specs=(P("group", "member", None), P("group", "member", None)),
        check_vma=False,
    )
```

```python
import jax
import jax.numpy as jnp
from jax import lax
from jax.experimental import pallas as pl
from jax.experimental.pallas import tpu as pltpu
from jax.sharding import PartitionSpec as P

ITERS = 3
ND = 768
LN = 128
NCH = ND // LN
DEV = 256
BASE = 16
F32 = jnp.float32
BF = jnp.bfloat16
NT = (((1,), (1,)), ((), ()))


def iota(shape, dim):
    return lax.broadcasted_iota(jnp.int32, shape, dim)


def coarse_kernel(
    load_hbm, node_hbm, map_hbm, sign_hbm, live_hbm, slot_hbm, count_hbm, coarse_hbm,
    modes_ref, pay_ref, load_ref, map_ref, sign_ref, live_ref, slot_ref, count_ref, coarse_ref,
    node_ref, sems,
):
    copies = [
        pltpu.make_async_copy(src, dst, sems.at[i])
        for i, (src, dst) in enumerate(
            (
                (node_hbm, node_ref), (load_hbm, load_ref), (map_hbm, map_ref), (sign_hbm, sign_ref),
                (live_hbm, live_ref), (slot_hbm, slot_ref), (count_hbm, count_ref),
                (coarse_hbm, coarse_ref),
            )
        )
    ]
    for c in copies:
        c.start()
    lane8 = iota((8, LN), 1)
    sub8 = iota((8, LN), 0)
    part = iota((8, ND), 0)
    row = jnp.zeros((1, LN), F32)
    dim = iota((1, ND), 1).astype(F32)
    node = jnp.floor((dim + 0.5) * (1.0 / 3.0))
    comp = dim - 3.0 * node
    first = (comp == 0.0).astype(F32)
    second = (comp == 1.0).astype(F32)
    third = (comp == 2.0).astype(F32)
    delta = iota((256, ND), 1) - 3 * iota((256, ND), 0)
    rep = jnp.where((delta >= 0) & (delta < 3), 1.0, 0.0).astype(BF)
    for c in copies[:2]:
        c.wait()
    for s in range(2):
        position = (node_ref[0, :, s, :].astype(F32) - 8.0) * 0.125
        spread = jnp.dot(position.astype(BF), rep, preferred_element_type=F32)
        cx = spread[0:1, :]
        cy = spread[1:2, :]
        cz = spread[2:3, :]
        rows = (
            first, second, third,
            third * cy - second * cz,
            first * cz - third * cx,
            second * cx - first * cy,
        )
        modes = jnp.zeros((8, ND), F32)
        for a in range(6):
            modes = jnp.where(part == a, rows[a], modes)
        modes_ref[s] = modes
        e = jnp.sum(modes * load_ref[0, s : s + 1, :], axis=1, keepdims=True)
        row = row + jnp.sum(jnp.where(lane8 == sub8 + 8 * s, e, 0.0), axis=0, keepdims=True)
    pay_ref[...] = jnp.broadcast_to(row, (DEV, LN))
    for c in copies[2:]:
        c.wait()


def tables_kernel(
    modes_ref, load_ref, map_ref, sign_ref, live_ref, slot_ref, count_ref, coarse_ref, l_hbm,
    tt_ref, qt_hbm, own_hbm, aux_ref, sib_ref, far_ref, g1_ref, g2_ref, d_ref,
    own_ref, qt_ref, sems, sems_d,
):
    blocks = [
        pltpu.make_async_copy(
            l_hbm.at[0, s, pl.ds(b * LN, LN), pl.ds(b * LN, LN)], d_ref.at[s * NCH + b], sems_d.at[s * NCH + b]
        )
        for s in range(2)
        for b in range(NCH)
    ]
    for c in blocks:
        c.start()
    part = iota((8, ND), 0)
    faces = []
    late = []
    for s in range(2):
        live = iota((1, ND), 1) < live_ref[0:1, s : s + 1]
        live_f = jnp.where(live, 1.0, 0.0)
        sgn = jnp.where(live, sign_ref[0, s : s + 1, :].astype(F32), 0.0)
        dof = map_ref[0, s : s + 1, :]
        dof_f = dof.astype(F32)
        high = jnp.floor(dof_f * (1.0 / 32.0))
        low = dof_f - 32.0 * high
        lhs = jnp.where(part == 0, high, jnp.where(part == 1, low, jnp.where(part == 2, sgn, 0.0)))
        pos64 = iota((1, 64), 1)
        slots = jnp.concatenate(
            [
                jnp.where(pos64 < count_ref[0, s : s + 1, f : f + 1], slot_ref[0, s, f : f + 1, :], -1)
                for f in range(4)
            ],
            axis=1,
        )
        hit = jnp.where(iota((ND, 256), 0) == slots, 1.0, 0.0).astype(BF)
        got = jnp.dot(lhs.astype(BF), hit, preferred_element_type=F32)
        dk = (32.0 * got[0:1, :] + got[1:2, :]).astype(jnp.int32)
        sk = got[2:3, :]
        tt = jnp.where(iota((ND, 256), 0) == dk, sk, 0.0)
        tt_b = tt.astype(BF)
        tt_ref[s] = tt_b
        qt = jnp.where(iota((ND, ND), 0) == dof, 1.0, 0.0).astype(BF)
        qt_ref[s] = qt
        qt_copy = pltpu.make_async_copy(qt_ref.at[s], qt_hbm.at[s], sems.at[1 + s])
        qt_copy.start()
        late.append(qt_copy)
        mask = lax.dot_general(
            jnp.broadcast_to(live_f, (8, ND)).astype(BF), qt, NT, preferred_element_type=F32
        )[0:1, :]
        count = lax.dot_general(
            jnp.ones((8, 256), BF), jnp.abs(tt).astype(BF), NT, preferred_element_type=F32
        )[0:1, :]
        aux_ref[s : s + 1, :] = mask
        aux_ref[2 + s : 3 + s, :] = mask * (1.0 - 0.5 * count)
        aux_ref[4 + s : 5 + s, :] = sgn
        aux_ref[6 + s : 7 + s, :] = load_ref[0, s : s + 1, :]
        modes = modes_ref[s]
        own_ref[s, 0:8, :] = modes * mask
        face = jnp.dot(modes.astype(BF), tt_b, preferred_element_type=F32)
        own_ref[s, 8:16, :] = jnp.concatenate([face, jnp.zeros((8, ND - 256), F32)], axis=1)
        faces.append(face)
    wide = 12 * DEV
    to_left, to_right, to_gm, to_gp = pack_faces(faces[0], faces[1])
    even_m = lax.axis_index("member") % 2 == 0
    even_g = lax.axis_index("group") % 2 == 0
    sib_ref[:, wide:] = jnp.where(even_m, to_right, to_left)
    far_ref[:, wide:] = jnp.where(even_m, to_left, to_right)
    zero = jnp.zeros((8, LN), F32)
    g1_ref[0:8, wide:] = jnp.where(even_g, to_gp, to_gm)
    g2_ref[0:8, wide:] = jnp.where(even_g, to_gm, to_gp)
    g1_ref[8:16, wide:] = zero
    g2_ref[8:16, wide:] = zero
    own_copy = pltpu.make_async_copy(own_ref, own_hbm, sems.at[0])
    own_copy.start()
    late.append(own_copy)
    perm = jnp.where(
        (iota((384, 384), 0) - 12 * (iota((384, 384), 1) % 32)) == iota((384, 384), 1) // 32, 1.0, 0.0
    ).astype(BF)
    keep = iota((8, 384), 0) < 6
    res = []
    for q in range(8):
        c = coarse_ref[:, 384 * q : 384 * (q + 1)]
        c16 = jnp.concatenate([c, jnp.zeros((4, 384), F32)], axis=0)
        up = jnp.where(keep, c16[0:8], 0.0)
        dn = jnp.where(keep, pltpu.roll(c16, 10, 0)[0:8], 0.0)
        both = jnp.concatenate([up, dn], axis=0)
        h = both.astype(BF)
        rest = both - h.astype(F32)
        m = rest.astype(BF)
        l = (rest - m.astype(F32)).astype(BF)
        got = jnp.dot(jnp.concatenate([h, m, l], axis=0), perm, preferred_element_type=F32)
        res.append(got[0:16] + got[16:32] + got[32:48])
    quarter = iota((16, LN), 1) // 32
    for v in range(12):
        for half in range(2):
            acc = None
            for i in range(4):
                src = res[4 * half + i][:, LN * (v // 4) : LN * (v // 4 + 1)]
                shift = (32 * (i - v % 4)) % LN
                src = pltpu.roll(src, shift, 1) if shift else src
                acc = src if acc is None else jnp.where(quarter == i, src, acc)
            at = v * DEV + half * LN
            sib_ref[:, at : at + LN] = jnp.where(even_m, acc[8:16], acc[0:8])
            far_ref[:, at : at + LN] = jnp.where(even_m, acc[0:8], acc[8:16])
            g1_ref[:, at : at + LN] = acc
            g2_ref[:, at : at + LN] = acc
    for c in late + blocks:
        c.wait()


def half_masks(rows):
    return iota((rows, LN), 1) < 64


def pack_faces(o0, o1):
    lo = half_masks(o0.shape[0])
    o0l, o0h, o1l, o1h = o0[:, :LN], o0[:, LN:], o1[:, :LN], o1[:, LN:]
    to_gm = jnp.where(lo, o0h, pltpu.roll(o1h, 64, 1))
    to_gp = jnp.where(lo, pltpu.roll(o0h, 64, 1), o1h)
    return o0l, o1l, to_gm, to_gp


def spread(near, own_ref, tt_ref, ar_ref):
    lo = half_masks(8)
    zero = jnp.zeros((8, LN), F32)
    left, right, gm, gp = near
    r0l, r1l = own_ref[0, 8:16, 0:LN], own_ref[1, 8:16, 0:LN]

    def both(a, b):
        return jnp.concatenate([a, b], axis=1)

    w0 = [
        both(zero, zero),
        both(pltpu.roll(jnp.where(lo, r1l, 0.0), 64, 1), zero),
        both(pltpu.roll(jnp.where(lo, 0.0, left), 64, 1), zero),
        both(zero, jnp.where(lo, gm, 0.0)),
        both(zero, jnp.where(lo, 0.0, pltpu.roll(gp, 64, 1))),
    ]
    w1 = [
        both(pltpu.roll(jnp.where(lo, 0.0, r0l), 64, 1), zero),
        both(zero, zero),
        both(pltpu.roll(jnp.where(lo, right, 0.0), 64, 1), zero),
        both(zero, jnp.where(lo, pltpu.roll(gm, 64, 1), 0.0)),
        both(zero, jnp.where(lo, 0.0, gp)),
    ]
    for s, w in ((0, w0), (1, w1)):
        table = jnp.concatenate(w, axis=0).astype(BF)
        ar_ref[s] = lax.dot_general(table, tt_ref[s], NT, preferred_element_type=F32)
        at = 8 * s
        ar_ref[s, at : at + 8, :] = own_ref[s, 0:8, :]


def two(a):
    h = a.astype(BF)
    return h, (a - h.astype(F32)).astype(BF)


def mm3(a, b):
    ah, al = two(a)
    bh, bl = two(b)

    def d(x, y):
        return jnp.dot(x, y, preferred_element_type=F32)

    return d(ah, bh) + (d(ah, bl) + d(al, bh))


def invert_kernel(l_hbm,diag_ref,out_hbm,out_ref,l_ref,d_ref,x_ref,sem_l,sem_o):
    copies_l=[pltpu.make_async_copy(l_hbm.at[0,s,pl.ds(b*LN,LN),pl.ds(0,b*LN)],l_ref.at[s,pl.ds(b*LN,LN),pl.ds(0,b*LN)],sem_l.at[s*NCH+b]) for s in range(2) for b in range(1,NCH)]
    for c in copies_l: c.start()
    ri=iota((LN,LN),0); ci=iota((LN,LN),1); eye=ri==ci; below=ri>ci
    lane=iota((BASE,LN),1); row=iota((BASE,LN),0)
    nb=2*NCH; ng=LN//BASE
    group=(lane//BASE)*BASE
    packs=[]
    for k in range(nb):
        lb=diag_ref[k]
        diag=jnp.sum(jnp.where(eye,lb,0.0),axis=1,keepdims=True)
        n=jnp.where(below,lb*(1.0/diag),0.0)
        rowdiag=jnp.sum(jnp.where(eye,lb,0.0),axis=0,keepdims=True)
        d_ref[k]=n
        x_ref[k,0:1,:]=1.0/rowdiag
        p=None
        for g in range(ng):
            t=jnp.where(lane//BASE==g,n[g*BASE:(g+1)*BASE,:],0.0)
            p=t if p is None else p+t
        packs.append(p)
    xs=[jnp.where(row==lane%BASE,1.0,0.0) for _ in range(nb)]
    for j in range(BASE-1):
        lo=(j+1)//8*8
        for k in range(nb):
            idx=group[lo:,:]+j
            f=jnp.take_along_axis(packs[k][lo:,:],idx,axis=1)
            new=xs[k][lo:,:]-f*xs[k][j:j+1,:]
            xs[k]=new if lo==0 else jnp.concatenate([xs[k][:lo,:],new],axis=0)
    invd=[x_ref[k,0:1,:] for k in range(nb)]
    for k in range(nb):
        for g in range(ng):
            x_ref[k,g*BASE:(g+1)*BASE,:]=jnp.where(lane//BASE==g,xs[k],0.0)
    z=jnp.zeros((LN,LN),F32)

    def bd(a,b):
        return jnp.concatenate([jnp.concatenate([a,z],axis=1),jnp.concatenate([z,b],axis=1)],axis=0)

    size=BASE
    while size<LN:
        pick=((ri//(2*size))==(ci//(2*size)))&((ri//size)!=(ci//size))
        ts=[]
        for q in range(nb//2):
            e=jnp.concatenate([jnp.where(pick,d_ref[2*q],0.0),jnp.where(pick,d_ref[2*q+1],0.0)],axis=1)
            ts.append(mm3(e,bd(x_ref[2*q],x_ref[2*q+1])))
        for q in range(nb//2):
            xc=jnp.concatenate([x_ref[2*q],x_ref[2*q+1]],axis=1)
            xn=xc-mm3(xc,bd(ts[q][:,:LN],ts[q][:,LN:]))
            x_ref[2*q]=xn[:,:LN]; x_ref[2*q+1]=xn[:,LN:]
        size*=2
    for k in range(nb): x_ref[k]=x_ref[k]*invd[k]
    for c in copies_l: c.wait()

    def block(s,i,j,w=LN): return l_ref[s,i*w:(i+1)*w,j*w:(j+1)*w]

    sent=[]

    def send_block(s,i,j):
        src=out_ref.at[s,pl.ds(i*2*LN,2*LN),pl.ds(j*2*LN,2*LN)]
        dst=out_hbm.at[s,pl.ds(i*2*LN,2*LN),pl.ds(j*2*LN,2*LN)]
        c=pltpu.make_async_copy(src,dst,sem_o.at[len(sent)])
        c.start()
        sent.append(c)

    pairs=[(s,q) for s in range(2) for q in range(NCH//2)]
    mids={}
    for s,q in pairs:
        mids[s,q]=mm3(block(s,2*q+1,2*q),x_ref[s*NCH+2*q])
    for s,q in pairs:
        at=2*q*LN
        out_ref[s,at:at+LN,at:at+LN]=x_ref[s*NCH+2*q]
        out_ref[s,at:at+LN,at+LN:at+2*LN]=z
        out_ref[s,at+LN:at+2*LN,at:at+LN]=-mm3(x_ref[s*NCH+2*q+1],mids[s,q])
        out_ref[s,at+LN:at+2*LN,at+LN:at+2*LN]=x_ref[s*NCH+2*q+1]
        send_block(s,q,q)
    wd=2*LN

    def inv(s,i,j): return out_ref[s,i*wd:(i+1)*wd,j*wd:(j+1)*wd]

    a=[[mm3(block(s,i,i-1,wd),inv(s,i-1,i-1)) for i in (1,2)] for s in range(2)]
    b=[mm3(block(s,2,0,wd),inv(s,0,0)) for s in range(2)]
    for s in range(2):
        for i in (1,2):
            out_ref[s,i*wd:(i+1)*wd,(i-1)*wd:i*wd]=-mm3(inv(s,i,i),a[s][i-1])
            send_block(s,i,i-1)
    for s in range(2):
        m=b[s]+mm3(block(s,2,1,wd),inv(s,1,0))
        out_ref[s,2*wd:3*wd,0:wd]=-mm3(inv(s,2,2),m)
        send_block(s,2,0)
    for c in sent: c.wait()


def split3(rows, total):
    idx = iota((total, rows[0].shape[1]), 0)
    out = jnp.zeros((total, rows[0].shape[1]), F32)
    for r, z in enumerate(rows):
        h = z.astype(BF).astype(F32)
        rest = z - h
        m = rest.astype(BF).astype(F32)
        l = rest - m
        out = jnp.where(idx == 3 * r, h, out)
        out = jnp.where(idx == 3 * r + 1, m, out)
        out = jnp.where(idx == 3 * r + 2, l, out)
    return out.astype(BF)


def solve(inv_ref, s, z):
    ys = []
    for b in range(NCH):
        acc = None
        for c in range(b + 1):
            term = inv_ref[s, b * LN : (b + 1) * LN, c * LN : (c + 1) * LN] * z[:, c * LN : (c + 1) * LN]
            acc = term if acc is None else acc + term
        ys.append(jnp.sum(acc, axis=1, keepdims=True))
    us = []
    for c in range(NCH):
        acc = None
        for b in range(c, NCH):
            term = inv_ref[s, b * LN : (b + 1) * LN, c * LN : (c + 1) * LN] * ys[b]
            acc = term if acc is None else acc + term
        us.append(jnp.sum(acc, axis=0, keepdims=True))
    return jnp.concatenate(us, axis=1)


def received_coarse(recv_ref):
    xt = jnp.transpose(recv_ref[...])

    def grp(i):
        return xt[8 * i : 8 * i + 8, :]

    h0 = grp(0) + pltpu.roll(grp(2), 1, 1) + pltpu.roll(grp(4), DEV - 16, 1) + pltpu.roll(grp(6), 16, 1)
    h1 = grp(1) + pltpu.roll(grp(3), DEV - 1, 1) + pltpu.roll(grp(5), DEV - 16, 1) + pltpu.roll(grp(7), 16, 1)
    sums = jnp.concatenate(
        [jnp.sum(grp(i), axis=1, keepdims=True)[6:8] for i in range(2)], axis=0
    )
    return h0, h1, sums


def project_rows(h0, h1, m_ref, ar_ref):
    acc = jnp.zeros((64, DEV), F32)
    for v in range(12):
        h = h0 if v < 6 else h1
        a = v % 6
        acc = acc + m_ref[:, v * DEV : (v + 1) * DEV] * h[a : a + 1, :]
    al = jnp.sum(acc, axis=1, keepdims=True)

    def grp(i):
        return al[8 * i : 8 * i + 8, :]

    a0 = jnp.concatenate([grp(0), grp(1), grp(3), grp(4), grp(6)], axis=0)
    a1 = jnp.concatenate([grp(0), grp(1), grp(2), grp(5), grp(7)], axis=0)
    w0 = jnp.sum(ar_ref[0] * a0, axis=0, keepdims=True)
    w1 = jnp.sum(ar_ref[1] * a1, axis=0, keepdims=True)
    return w0, w1


def places():
    g = lax.axis_index("group")
    m = lax.axis_index("member")
    me = g * 16 + m
    sib = me + 1 - 2 * (m % 2)
    return (
        jnp.where(m > 0, me - 1, me),
        jnp.where(m < 15, me + 1, me),
        jnp.where(g > 0, me - 16, me),
        jnp.where(g < 15, me + 16, me),
        jnp.where(g > 0, sib - 16, me),
        jnp.where(g < 15, sib + 16, me),
    )


def tile_of(row):
    base = pl.multiple_of((row // 8) * 8, 8)
    return base, row - base


def face_row(recv_ref, row):
    base, offset = tile_of(row)
    tile = recv_ref[pl.ds(base, 8), :]
    return jnp.sum(jnp.where(iota((8, LN), 0) == offset, tile, 0.0), axis=0, keepdims=True)


def assembled(recv_ref, y, o, tt_ref):
    lo = half_masks(1)
    left, right, gm, gp, sgm, sgp = (face_row(recv_ref, row) for row in places())
    o0l, o1l = o[0][:, :LN], o[1][:, :LN]
    in0 = jnp.concatenate(
        [pltpu.roll(jnp.where(lo, o1l, left), 64, 1), jnp.where(lo, pltpu.roll(gm, 64, 1), gp)], axis=1
    )
    in1 = jnp.concatenate(
        [jnp.where(lo, pltpu.roll(o0l, 64, 1), right), jnp.where(lo, pltpu.roll(sgm, 64, 1), sgp)], axis=1
    )
    out = []
    for s, inc in ((0, in0), (1, in1)):
        add = lax.dot_general(split3([inc], 8), tt_ref[s], NT, preferred_element_type=F32)
        out.append(y[s] + jnp.sum(add, axis=0, keepdims=True))
    return out


def faces_of(y, tt_ref):
    o = []
    for s in range(2):
        prod = jnp.dot(split3([y[s]], 8), tt_ref[s], preferred_element_type=F32)
        o.append(jnp.sum(prod, axis=0, keepdims=True))
    return o


def make_coef(count):
    def coef_kernel(st_ref, ar_ref, aux_ref, row_ref):
        y = pair(st_ref, YV)
        c0, c1 = (jnp.sum(ar_ref[s] * y[s], axis=1, keepdims=True) for s in range(2))

        def grp(c, i):
            return c[8 * i : 8 * i + 8, :]

        cc = jnp.concatenate(
            [
                grp(c0, 0) + grp(c1, 0), grp(c0, 1) + grp(c1, 1), grp(c1, 2), grp(c0, 2),
                grp(c0, 3), grp(c1, 3), grp(c0, 4), grp(c1, 4),
            ],
            axis=0,
        )
        diag = iota((64, LN), 0) == iota((64, LN), 1)
        row = jnp.sum(jnp.where(diag, cc, 0.0), axis=0, keepdims=True)
        lane = iota((1, LN), 1)
        dots = []
        if count >= 2:
            p = pair(st_ref, PV)
            weight = pair(aux_ref, 2)
            dots = [inner([weight[s] * p[s] for s in range(2)], p), inner(p, y)]
        if count >= 4:
            dots += [inner(pair(st_ref, DV), y), inner(p, pair(st_ref, YD))]
        for at, value in zip((6, 7, 14, 15), dots):
            row = jnp.where(lane == at, value, row)
        row_ref[...] = jnp.broadcast_to(row, (8, LN))

    return coef_kernel


def pay_kernel(row_ref, sib_ref, o_ref, pay_ref):
    pay_ref[...] = jnp.broadcast_to(row_ref[0:1, :], (DEV, LN))
    o0l, o0h, o1l = o_ref[0:1, 0:LN], o_ref[0:1, LN : 2 * LN], o_ref[1:2, 0:LN]
    other = sib_ref[1:2, LN : 2 * LN]
    faces = (pltpu.roll(o0l, 64, 1), o1l, pltpu.roll(o0h, 64, 1), o0h, pltpu.roll(other, 64, 1), other)
    for row, face in zip(places(), faces):
        base, offset = tile_of(row)
        old = pay_ref[pl.ds(base, 8), :]
        put_here = (iota((8, LN), 0) == offset) & (iota((8, LN), 1) >= 64)
        pay_ref[pl.ds(base, 8), :] = jnp.where(put_here, face, old)


def inner(a, b):
    return jnp.sum(a[0] * b[0] + a[1] * b[1], axis=1, keepdims=True)


def pair(ref, i):
    return [ref[i : i + 1, :], ref[i + 1 : i + 2, :]]


def put(ref, i, v):
    ref[i : i + 1, :] = v[0]
    ref[i + 1 : i + 2, :] = v[1]


LAM, PV, DV, IM, YD, YV = 0, 2, 4, 6, 8, 10


def begin_kernel(
    recv_ref, tt_ref, aux_ref, inv_hbm, own_hbm, mine_ref, near_ref,
    ar_ref, m_ref, st_ref, o_ref, inv_ref, own_ref, sems, sems_inv,
):
    wide = 12 * DEV
    own_copy = pltpu.make_async_copy(own_hbm, own_ref, sems.at[0])
    own_copy.start()
    parts = [
        pltpu.make_async_copy(
            inv_hbm.at[s, pl.ds(b * LN, LN), pl.ds(0, (b + 1) * LN)],
            inv_ref.at[s, pl.ds(b * LN, LN), pl.ds(0, (b + 1) * LN)],
            sems_inv.at[s * NCH + b],
        )
        for s in range(2)
        for b in range(NCH)
    ]
    for c in parts:
        c.start()
    h0, h1, _ = received_coarse(recv_ref)
    m_ref[0:16, :] = mine_ref[:, 0:wide]
    even_m = lax.axis_index("member") % 2 == 0
    even_g = lax.axis_index("group") % 2 == 0
    sib, far = near_ref[0:8, :], near_ref[8:16, :]
    first, second = near_ref[16:32, :], near_ref[32:48, :]
    right = jnp.where(even_m, sib, far)
    left = jnp.where(even_m, far, sib)
    gm = jnp.where(even_g, second, first)
    gp = jnp.where(even_g, first, second)
    m_ref[16:24, :] = right[:, 0:wide]
    m_ref[24:32, :] = left[:, 0:wide]
    m_ref[32:48, :] = gm[:, 0:wide]
    m_ref[48:64, :] = gp[:, 0:wide]
    own_copy.wait()
    near = [left[:, wide:], right[:, wide:], gm[0:8, wide:], gp[0:8, wide:]]
    spread(near, own_ref, tt_ref, ar_ref)
    lam = project_rows(h0, h1, m_ref, ar_ref)
    mask = pair(aux_ref, 0)
    load = pair(aux_ref, 6)
    for c in parts:
        c.wait()
    y = [mask[s] * solve(inv_ref, s, load[s] - lam[s]) for s in range(2)]
    o = faces_of(y, tt_ref)
    put(st_ref, LAM, lam)
    put(st_ref, YV, y)
    put(o_ref, 0, o)


def next_solve(inv_ref, tt_ref, aux_ref, p):
    mask = pair(aux_ref, 0)
    y = [mask[s] * solve(inv_ref, s, p[s]) for s in range(2)]
    return y, faces_of(y, tt_ref)


def first_kernel(recv_ref, st_ref, o_ref, inv_ref, tt_ref, ar_ref, m_ref, aux_ref, st2_ref, o2_ref):
    h0, h1, _ = received_coarse(recv_ref)
    w = project_rows(h0, h1, m_ref, ar_ref)
    res = assembled(recv_ref, pair(st_ref, YV), pair(o_ref, 0), tt_ref)
    p = [res[s] - w[s] for s in range(2)]
    y, o = next_solve(inv_ref, tt_ref, aux_ref, p)
    put(st2_ref, LAM, pair(st_ref, LAM))
    put(st2_ref, PV, p)
    put(st2_ref, YV, y)
    put(o2_ref, 0, o)


def step_body(it, recv_ref, st_ref, o_ref, hs_ref, tt_ref, ar_ref, m_ref):
    h0, h1, sums = received_coarse(recv_ref)
    norm = sums[0:1, :]
    y = pair(st_ref, YV)
    p = pair(st_ref, PV)
    image = assembled(recv_ref, y, pair(o_ref, 0), tt_ref)
    if it == 0:
        d, yd, curve = p, y, sums[1:2, :]
    else:
        beta = norm / hs_ref[16:17, 0:1]
        curve = sums[1:2, :] + beta * (sums[2:3, :] + sums[3:4, :]) + beta * beta * hs_ref[17:18, 0:1]
        dold, iold, yold = pair(st_ref, DV), pair(st_ref, IM), pair(st_ref, YD)
        d = [p[s] + beta * dold[s] for s in range(2)]
        yd = [y[s] + beta * yold[s] for s in range(2)]
        image = [image[s] + beta * iold[s] for s in range(2)]
        h0 = h0 + beta * hs_ref[0:8, :]
        h1 = h1 + beta * hs_ref[8:16, :]
    step = norm / curve
    w = project_rows(h0, h1, m_ref, ar_ref)
    lam = pair(st_ref, LAM)
    lam = [lam[s] + step * d[s] for s in range(2)]
    pn = [p[s] - step * (image[s] - w[s]) for s in range(2)]
    return lam, pn, d, yd, image, h0, h1, norm, curve


def make_step(it):
    def step_kernel(
        recv_ref, st_ref, o_ref, hs_ref, inv_ref, tt_ref, ar_ref, m_ref, aux_ref,
        st2_ref, o2_ref, hs2_ref,
    ):
        lam, pn, d, yd, image, h0, h1, norm, curve = step_body(
            it, recv_ref, st_ref, o_ref, hs_ref, tt_ref, ar_ref, m_ref
        )
        y, o = next_solve(inv_ref, tt_ref, aux_ref, pn)
        for at, v in ((LAM, lam), (PV, pn), (DV, d), (IM, image), (YD, yd), (YV, y)):
            put(st2_ref, at, v)
        put(o2_ref, 0, o)
        hs2_ref[0:8, :] = h0
        hs2_ref[8:16, :] = h1
        hs2_ref[16:17, :] = jnp.broadcast_to(norm, (1, DEV))
        hs2_ref[17:18, :] = jnp.broadcast_to(curve, (1, DEV))

    return step_kernel


def last_kernel(recv_ref, st_ref, o_ref, hs_ref, tt_ref, ar_ref, m_ref, aux_ref, qt_ref, lam_ref, p_ref):
    lam, pn = step_body(ITERS - 1, recv_ref, st_ref, o_ref, hs_ref, tt_ref, ar_ref, m_ref)[:2]
    for s in range(2):
        got = jnp.dot(split3([lam[s], pn[s]], 8), qt_ref[s], preferred_element_type=F32)
        sgn = aux_ref[4 + s : 5 + s, :]
        lam_ref[s : s + 1, :] = sgn * jnp.sum(got[0:3, :], axis=0, keepdims=True)
        p_ref[s : s + 1, :] = sgn * jnp.sum(got[3:6, :], axis=0, keepdims=True)


def sds(shape, dtype=F32):
    return jax.ShapeDtypeStruct(shape, dtype)


VM = pl.BlockSpec(memory_space=pltpu.VMEM)
HB = pl.BlockSpec(memory_space=pltpu.HBM)


def call(kernel, outs, specs, *args, scratch=(), flops=0, mib=16, hbm_outs=()):
    args = [
        pltpu.with_memory_space_constraint(x, pltpu.HBM) if specs.get(i) is HB else x for i, x in enumerate(args)
    ]
    return pl.pallas_call(
        kernel,
        out_shape=outs,
        in_specs=[specs.get(i, VM) for i in range(len(args))],
        out_specs=tuple(HB if i in hbm_outs else VM for i in range(len(outs))),
        scratch_shapes=list(scratch),
        compiler_params=pltpu.CompilerParams(vmem_limit_bytes=mib * 2**20),
        cost_estimate=pl.CostEstimate(flops=flops, transcendentals=0, bytes_accessed=2**20)
        if flops
        else None,
    )(*args)


def shards(factor, load, dof_map, dof_sign, live_count, face_slot, face_count, node_coord, coarse_inverse):
    axes = ("group", "member")
    packed = 12 * DEV + LN
    raw = (load, dof_map, dof_sign, live_count, face_slot, face_count, coarse_inverse)
    modes, pay0, *raw = call(
        coarse_kernel,
        (sds((2, 8, ND)), sds((DEV, LN))) + tuple(sds(r.shape, r.dtype) for r in raw),
        {i: HB for i in range(8)},
        load, node_coord.transpose(0, 2, 1, 3), *raw[1:],
        scratch=[pltpu.VMEM((1, 3, 2, 256), node_coord.dtype), pltpu.SemaphoreType.DMA((8,))],
    )

    def exchange(pay):
        return lax.all_to_all(pay, axes, 0, 0, tiled=True)

    recv0 = exchange(pay0)
    tt, qt, own, aux, to_sib, to_far, to_g1, to_g2, diag = call(
        tables_kernel,
        (
            sds((2, ND, 256), BF), pltpu.HBM((2, ND, ND), BF), pltpu.HBM((2, 16, ND), F32), sds((8, ND)),
            sds((8, packed)), sds((8, packed)), sds((16, packed)), sds((16, packed)), sds((2 * NCH, LN, LN)),
        ),
        {8: HB},
        modes, *raw, factor,
        scratch=[
            pltpu.VMEM((2, 16, ND), F32), pltpu.VMEM((2, ND, ND), BF),
            pltpu.SemaphoreType.DMA((3,)), pltpu.SemaphoreType.DMA((2 * NCH,)),
        ],
        hbm_outs=(1, 2),
    )

    swap = [(i, i ^ 1) for i in range(16)]
    cross = [(i, ((i + 1) ^ 1) - 1) for i in range(1, 15)]
    from_g1 = lax.ppermute(to_g1, "group", swap)
    from_g2 = lax.ppermute(to_g2, "group", cross)
    from_far = lax.ppermute(to_far, "member", cross)
    from_sib = lax.ppermute(to_sib, "member", swap)
    (inv,) = call(
        invert_kernel,
        (pltpu.HBM((2, ND, ND), F32),),
        {0: HB},
        factor, diag,
        scratch=[
            pltpu.VMEM((2, ND, ND), F32), pltpu.VMEM((2, ND, ND), F32), pltpu.VMEM((2 * NCH, LN, LN), F32),
            pltpu.VMEM((2 * NCH, LN, LN), F32), pltpu.SemaphoreType.DMA((2 * NCH,)),
            pltpu.SemaphoreType.DMA((2 * NCH,)),
        ],
        hbm_outs=(0,),
        flops=20_000_000_000,
        mib=24,
    )
    near = jnp.concatenate([from_sib, from_far, from_g1, from_g2], axis=0)
    st_s, o_s, hs_s = sds((12, ND)), sds((2, 256)), sds((24, DEV))

    def gather(count, st, o):
        other = lax.ppermute(o, "member", swap)
        (row,) = call(make_coef(count), (sds((8, LN)),), {}, st, ar, aux)
        (pay,) = call(pay_kernel, (sds((DEV, LN)),), {}, row, other, o)
        return exchange(pay)

    ar, table, st, o = call(
        begin_kernel,
        (sds((2, 40, ND)), sds((64, 12 * DEV)), st_s, o_s),
        {3: HB, 4: HB},
        recv0, tt, aux, inv, own, to_g1, near,
        scratch=[
            pltpu.VMEM((2, ND, ND), F32), pltpu.VMEM((2, 16, ND), F32),
            pltpu.SemaphoreType.DMA((1,)), pltpu.SemaphoreType.DMA((2 * NCH,)),
        ],
    )
    st, o = call(first_kernel, (st_s, o_s), {}, gather(0, st, o), st, o, inv, tt, ar, table, aux)
    hs = jnp.zeros((24, DEV), F32)
    for it in range(ITERS - 1):
        st, o, hs = call(
            make_step(it), (st_s, o_s, hs_s), {},
            gather(4 if it else 2, st, o), st, o, hs, inv, tt, ar, table, aux,
        )
    lam, proj = call(
        last_kernel, (sds((2, ND)), sds((2, ND))), {},
        gather(4, st, o), st, o, hs, tt, ar, table, aux, qt,
    )
    return lam[None], proj[None]


def solution(mesh):
    return jax.shard_map(
        shards,
        mesh=mesh,
        in_specs=(
            P("group", "member", None, None),
            P("group", "member", None),
            P("group", "member", None),
            P("group", "member", None),
            P("group", "member"),
            P("group", "member", None, None),
            P("group", "member", None),
            P("group", "member", None, None),
            P(("group", "member"), None),
        ),
        out_specs=(P("group", "member", None), P("group", "member", None)),
        check_vma=False,
    )
```
